32 devices in a mesh: groups: 2 (over x), samp: 8 (over z, y), line: 2 (over core).
Axes of the slice: x: 2, y: 2, z: 4, core: 2. Of those that a mesh axis runs over, the one named last changes fastest.
Arguments:
- cube: float32 [7077888], P(('groups', 'samp', 'line')), parts along dimension 0, may hold values from -4000 to 4000
Outputs:
- details1: float32 [5308416], P(('groups', 'samp', 'line')), parts along dimension 0
- details2: float32 [1327104], P(('groups', 'samp', 'line')), parts along dimension 0
- details3: float32 [331776], P(('groups', 'samp', 'line')), parts along dimension 0
- approx: float32 [110592], P(('groups', 'samp', 'line')), parts along dimension 0
The draws below stay inside these ranges and needn't reach their ends.
There are 2 independent parts, one for each index of `groups`. The reference program is written for one: setup_inputs(seed, part) draws one part's arguments, and reference() takes and returns one part's arrays. A program takes and returns all parts, laid end to end along the dimension named above; each array names one. Nothing has to cross between parts.
All inputs are finite; a program needn't handle non-finite values.
Results may differ from the reference program's by a relative error of at most 0.000088.
Values sent between devices are 32-bit elements; how exact they have to be, the bound alone decides.
A program may use at most 64 MiB of HBM per device.

```python
import math
import jax
import jax.numpy as jnp
from jax import lax

BANDS = 432
LD = 32
SD = 16
LINES = 64
SAMPLES = 128
NPIX = 8192
N_SAMP = 8
N_LINE = 2


def draw_cube(key, part):
    subkeys = jax.random.split(key, 4)
    log_ten = math.log(10.0)
    band_scale = jnp.exp(jax.random.uniform(subkeys[0], (BANDS, 1, 1), jnp.float32, 0.0, log_ten))
    offset = jax.random.uniform(subkeys[1], (BANDS, 1, 1), jnp.float32, -1.0, 1.0)
    sample_ramp = 1.0 + 2.0 * jnp.arange(SAMPLES, dtype=jnp.float32) / (SAMPLES - 1)
    pixel_scale = jnp.exp(jax.random.uniform(subkeys[2], (1, LINES, SAMPLES), jnp.float32, 0.0, log_ten)) * sample_ramp
    fresh_noise = jnp.clip(jax.random.normal(subkeys[3], (BANDS, LINES, SAMPLES), jnp.float32), -4.0, 4.0)
    common = jnp.zeros((1, LINES, SAMPLES), jnp.float32)
    blended = fresh_noise + 0.6 * jnp.roll(fresh_noise, 1, 0) + 0.4 * jnp.roll(fresh_noise, 2, 0)
    image = band_scale * (offset + common + pixel_scale * blended)
    shaped = image.reshape(BANDS, LINES // LD, LD, SAMPLES // SD, SD)
    return jnp.transpose(shaped, (3, 1, 0, 2, 4)).reshape(-1)


def setup_inputs(seed: int = 0, part: int = 0) -> dict:
    splits = jax.random.split(jax.random.key(seed), 2)
    part_splits = jax.random.split(jax.random.fold_in(splits[1], part), 2)
    return {
        "cube": draw_cube(jax.random.fold_in(jax.random.fold_in(splits[1], part), 71), part),
    }


alpha_lift = -1.586134342059924
beta_lift = -0.052980118572961
gamma_lift = 0.882911075530934
delta_lift = 0.443506852043971
scale_lift = 1.230174104914001

def split_pairs(values, axis):
    length = values.shape[axis]
    return (lax.slice_in_dim(values, 0, length, 2, axis), lax.slice_in_dim(values, 1, length, 2, axis))

def lift(values, axis):
    evens, odds = split_pairs(values, axis)
    half = evens.shape[axis]
    for weight_odd, weight_even in ((alpha_lift, beta_lift), (gamma_lift, delta_lift)):
        following = jnp.concatenate([lax.slice_in_dim(evens, 1, half, 1, axis), lax.slice_in_dim(evens, half - 1, half, 1, axis)], axis)
        odds = odds + weight_odd * (evens + following)
        preceding = jnp.concatenate([lax.slice_in_dim(odds, 0, 1, 1, axis), lax.slice_in_dim(odds, 0, half - 1, 1, axis)], axis)
        evens = evens + weight_even * (preceding + odds)
    return (evens / scale_lift, odds * scale_lift)

def subbands(values):
    low_s, high_s = lift(values, 2)
    low_l, high_l = lift(jnp.concatenate([low_s, high_s], 2), 1)
    middle = low_s.shape[2]
    details = jnp.stack([high_l[:, :, :middle], low_l[:, :, middle:], high_l[:, :, middle:]])
    return (low_l[:, :, :middle], details)

def to_tiles(values, level):
    tile_lines = LD // level
    tile_samples = SD // level
    lead = values.shape[:-2]
    count = len(lead)
    shaped = values.reshape(lead + (N_LINE, tile_lines, N_SAMP, tile_samples))
    order = (count + 2, count) + tuple(range(count)) + (count + 1, count + 3)
    return jnp.transpose(shaped, order).reshape(-1)

def reference(cube):
    tiled = cube.reshape(N_SAMP, N_LINE, BANDS, LD, SD)
    image = jnp.transpose(tiled, (2, 1, 3, 0, 4)).reshape(BANDS, LD * N_LINE, SD * N_SAMP)
    band_count = BANDS
    flattened = image.reshape(band_count, -1)
    band_mean = jnp.sum(flattened, axis=1) / NPIX
    centered = flattened - band_mean[:, None]
    covariance = jnp.dot(centered.astype(jnp.float32), centered.T.astype(jnp.float32), precision=lax.Precision.HIGHEST, preferred_element_type=jnp.float32) / NPIX
    identity = jnp.eye(band_count, dtype=covariance.dtype)
    regular = covariance + 0.01 * (jnp.trace(covariance) / band_count) * identity
    factor = jnp.linalg.cholesky(regular)
    whitener = lax.linalg.triangular_solve(factor, identity, left_side=True, lower=True)
    components = jnp.dot(whitener.astype(jnp.float32), centered.astype(jnp.float32), precision=lax.Precision.HIGHEST, preferred_element_type=jnp.float32).reshape(image.shape)
    approx1, level1 = subbands(components)
    approx2, level2 = subbands(approx1)
    approx3, level3 = subbands(approx2)
    return (to_tiles(level1, 2), to_tiles(level2, 4), to_tiles(level3, 8), to_tiles(approx3, 8))
```

```python
import functools
import jax
import jax.numpy as jnp
from jax import lax
from jax.experimental import pallas as pl
from jax.experimental.pallas import tpu as pltpu
from jax.sharding import PartitionSpec as P

MESH = pl.DeviceIdType.MESH
HIGH = lax.Precision.HIGHEST
LANES = 128


def blocks_of(bands):
    rows = [bands - start for start in range(0, bands, LANES)]
    offsets = [sum(rows[:i]) for i in range(len(rows))]
    return rows, offsets


def gram_kernel(samp, line, bands, pixels, x_ref, xc_ref, p_ref, xs, sums, sums_in, g, half_in,
                chunk_in, tot, s_send, s_recv, h_send, h_recv, c_send, c_recv, a_send, a_recv,
                b_send, b_recv):
    me, ln = lax.axis_index("samp"), lax.axis_index("line")
    devices = samp * line
    flat = me * line + ln
    packs = pixels // LANES
    padded = xs.shape[0]

    def peer(d):
        other = lax.rem(flat + d, devices)
        return {"samp": other // line, "line": lax.rem(other, line)}

    barrier = pltpu.get_barrier_semaphore()
    for d in range(1, devices):
        pl.semaphore_signal(barrier, inc=1, device_id=peer(d), device_id_type=MESH)
    if padded > bands:
        xs[bands:, :] = jnp.zeros((padded - bands, pixels), jnp.float32)
    for q in range(packs):
        xs[0:bands, q * LANES:(q + 1) * LANES] = x_ref[pl.ds(q, bands, stride=packs), :]
    sums[...] = lax.dot_general(jnp.ones((8, pixels), jnp.float32), xs[...], (((1,), (1,)), ((), ())),
                                precision=HIGH, preferred_element_type=jnp.float32)
    pl.semaphore_wait(barrier, devices - 1)
    copies = []
    for d in range(1, devices):
        copy = pltpu.make_async_remote_copy(sums, sums_in.at[d - 1], s_send.at[d - 1], s_recv.at[d - 1],
                                            device_id=peer(d), device_id_type=MESH)
        copy.start()
        copies.append(copy)
    for copy in copies:
        copy.wait()
    total = sums[...]
    for d in range(1, devices):
        total = total + sums_in[d - 1]
    mean = jnp.transpose(total / float(pixels * devices))[:, 0:1]
    xs[...] = xs[...] - mean
    xc_ref[...] = xs[0:bands, :]
    rows, offsets = blocks_of(bands)
    for q, (count, offset) in enumerate(zip(rows, offsets)):
        g[offset:offset + count, :] = lax.dot_general(
            xs[q * LANES:q * LANES + count, :], xs[q * LANES:(q + 1) * LANES, :],
            (((1,), (1,)), ((), ())), precision=HIGH, preferred_element_type=jnp.float32)
    used = offsets[-1] + rows[-1]
    if g.shape[0] > used:
        g[used:, :] = jnp.zeros((g.shape[0] - used, LANES), jnp.float32)
    half = g.shape[0] // line
    chunk = half // samp
    copies = []
    for d in range(1, line):
        other = lax.rem(ln + d, line)
        copy = pltpu.make_async_remote_copy(
            g.at[pl.ds(pl.multiple_of(other * half, 8), half)], half_in.at[d - 1], h_send.at[d - 1],
            h_recv.at[d - 1], device_id={"line": other}, device_id_type=MESH)
        copy.start()
        copies.append(copy)
    for copy in copies:
        copy.wait()
    mine = pl.ds(pl.multiple_of(ln * half, 8), half)
    value = g[mine, :]
    for d in range(1, line):
        value = value + half_in[d - 1]
    g[mine, :] = value
    copies = []
    for d in range(1, samp):
        other = lax.rem(me + d, samp)
        copy = pltpu.make_async_remote_copy(
            g.at[pl.ds(pl.multiple_of(ln * half + other * chunk, 8), chunk)], chunk_in.at[d - 1],
            c_send.at[d - 1], c_recv.at[d - 1], device_id={"samp": other}, device_id_type=MESH)
        copy.start()
        copies.append(copy)
    for copy in copies:
        copy.wait()
    own = pl.ds(pl.multiple_of(ln * half + me * chunk, 8), chunk)
    value = g[own, :]
    for d in range(1, samp):
        value = value + chunk_in[d - 1]
    tot[own, :] = value
    copies = []
    for d in range(1, samp):
        other = lax.rem(me + d, samp)
        copy = pltpu.make_async_remote_copy(tot.at[own], tot.at[own], a_send.at[d - 1], a_recv.at[d - 1],
                                            device_id={"samp": other}, device_id_type=MESH)
        copy.start()
        copies.append(copy)
    for copy in copies:
        copy.wait()
    copies = []
    for d in range(1, line):
        other = lax.rem(ln + d, line)
        copy = pltpu.make_async_remote_copy(tot.at[mine], tot.at[mine], b_send.at[d - 1], b_recv.at[d - 1],
                                            device_id={"line": other}, device_id_type=MESH)
        copy.start()
        copies.append(copy)
    for copy in copies:
        copy.wait()
    p_ref[...] = tot[...]


def gram_call(cube, bands, pixels):
    samp, line = lax.axis_size("samp"), lax.axis_size("line")
    devices = samp * line
    rows, offsets = blocks_of(bands)
    used = offsets[-1] + rows[-1]
    unit = 8 * devices
    total = -(-used // unit) * unit
    padded = -(-bands // LANES) * LANES
    f32 = jnp.float32
    sem = pltpu.SemaphoreType.DMA
    return pl.pallas_call(
        functools.partial(gram_kernel, samp, line, bands, pixels),
        out_shape=(jax.ShapeDtypeStruct((bands, pixels), f32), jax.ShapeDtypeStruct((total, LANES), f32)),
        in_specs=[pl.BlockSpec(memory_space=pltpu.VMEM)],
        out_specs=(pl.BlockSpec(memory_space=pltpu.VMEM), pl.BlockSpec(memory_space=pltpu.VMEM)),
        scratch_shapes=[
            pltpu.VMEM((padded, pixels), f32), pltpu.VMEM((8, padded), f32),
            pltpu.VMEM((devices - 1, 8, padded), f32), pltpu.VMEM((total, LANES), f32),
            pltpu.VMEM((line - 1, total // line, LANES), f32),
            pltpu.VMEM((samp - 1, total // devices, LANES), f32), pltpu.VMEM((total, LANES), f32),
            sem((devices - 1,)), sem((devices - 1,)), sem((line - 1,)), sem((line - 1,)),
            sem((samp - 1,)), sem((samp - 1,)), sem((samp - 1,)), sem((samp - 1,)),
            sem((line - 1,)), sem((line - 1,)),
        ],
        compiler_params=pltpu.CompilerParams(collective_id=0, has_side_effects=True),
    )(cube.reshape(-1, LANES))


def split3(value):
    first = value.astype(jnp.bfloat16).astype(jnp.float32)
    rest = value - first
    second = rest.astype(jnp.bfloat16).astype(jnp.float32)
    return first, second, rest - second


def inverse_kernel(bands, count, p_ref, w_ref, m):
    wide = m.shape[1]
    rows, offsets = blocks_of(bands)
    diag = lax.broadcasted_iota(jnp.int32, (LANES, LANES), 0) == lax.broadcasted_iota(
        jnp.int32, (LANES, LANES), 1)
    scale = 1.0 / float(count)
    trace = jnp.zeros((1, 1), jnp.float32)
    for q, offset in enumerate(offsets):
        size = min(LANES, rows[q])
        block = p_ref[offset:offset + size, :]
        kept = jnp.where(diag[:size], block, 0.0)
        trace = trace + jnp.sum(jnp.sum(kept, axis=0, keepdims=True), axis=1, keepdims=True)
    ridge = trace * scale * (0.01 / bands)
    for q, offset in enumerate(offsets):
        for b in range(q, len(rows)):
            size = min(LANES, rows[b])
            start = offset + (b - q) * LANES
            block = p_ref[start:start + size, :] * scale
            if b == q:
                low = jnp.where(diag[:size], block + ridge, block)
                m[q * LANES:q * LANES + size, q * LANES:(q + 1) * LANES] = low
            else:
                if size < LANES:
                    block = jnp.concatenate([block, jnp.zeros((LANES - size, LANES), jnp.float32)], axis=0)
                m[q * LANES:(q + 1) * LANES, b * LANES:(b + 1) * LANES] = jnp.transpose(block)
                m[b * LANES:b * LANES + size, q * LANES:(q + 1) * LANES] = block[:size]
    sub = lax.broadcasted_iota(jnp.int32, (8, LANES), 0)
    lane = lax.broadcasted_iota(jnp.int32, (8, LANES), 1)

    for c in range(len(rows)):
        top = c * LANES
        span = bands - top

        def step(j, carry):
            row = pl.multiple_of(top + 8 * j, 8)
            here = m[pl.ds(row, 8), top:top + LANES]
            small = pltpu.roll(here, lax.rem(LANES - 8 * j, LANES), 1)
            columns = [jnp.broadcast_to(small[:, b:b + 1], (8, LANES)) for b in range(8)]
            d = [[jnp.broadcast_to(columns[b][a:a + 1, :], (8, LANES)) if b <= a else None
                  for b in range(8)] for a in range(8)]
            low = [[None] * 8 for _ in range(8)]
            root = [None] * 8
            for b in range(8):
                root[b] = lax.rsqrt(d[b][b])
                for a in range(b + 1, 8):
                    low[a][b] = d[a][b] * root[b]
                for a in range(b + 1, 8):
                    for e in range(b + 1, a + 1):
                        d[a][e] = d[a][e] - low[a][b] * low[e][b]
            inv = [[None] * 8 for _ in range(8)]
            for b in range(8):
                inv[b][b] = root[b]
                for a in range(b + 1, 8):
                    acc = low[a][b] * inv[b][b]
                    for e in range(b + 1, a):
                        acc = acc + low[a][e] * inv[e][b]
                    inv[a][b] = -(acc * root[a])
            wcol = []
            for b in range(8):
                col = jnp.where(sub == b, inv[b][b], 0.0)
                for a in range(b + 1, 8):
                    col = jnp.where(sub == a, inv[a][b], col)
                wcol.append(col)
            tiles = []
            for t in range(wide // LANES):
                acc = None
                panel = m[pl.ds(row, 8), t * LANES:(t + 1) * LANES]
                for b in range(8):
                    term = wcol[b] * panel[b:b + 1, :]
                    acc = term if acc is None else acc + term
                if t == c:
                    for b in range(8):
                        acc = jnp.where(lane == 8 * j + b, wcol[b], acc)
                tiles.append(acc)
            r = jnp.concatenate(tiles, axis=1)
            m[pl.ds(row, 8), :] = r
            one, two, three = split3(r)
            right = jnp.concatenate([one, two, three, one, two, one], axis=0)
            cols = lax.broadcasted_iota(jnp.int32, (8, wide), 1)
            keep = (cols >= row + 8).astype(jnp.float32)
            l1, l2, l3 = one * keep, two * keep, three * keep
            left = jnp.concatenate([l1, l1, l1, l2, l2, l3], axis=0)[:, top:]
            update = lax.dot_general(
                jnp.transpose(left).astype(jnp.bfloat16), right.astype(jnp.bfloat16),
                (((1,), (0,)), ((), ())), preferred_element_type=jnp.float32)
            for t in range(wide // LANES):
                part = slice(t * LANES, (t + 1) * LANES)
                old = m[top:bands, part]
                if t == c:
                    line_ids = lax.broadcasted_iota(jnp.int32, (span, LANES), 0)
                    lane_ids = lax.broadcasted_iota(jnp.int32, (span, LANES), 1)
                    inside = (lane_ids >= 8 * j) & (lane_ids < 8 * j + 8) & (line_ids >= 8 * j + 8)
                    old = jnp.where(inside, 0.0, old)
                m[top:bands, part] = old - update[:span, part]
            return carry

        lax.fori_loop(0, min(LANES, span) // 8, step, 0)
    keep = lax.broadcasted_iota(jnp.int32, (bands, wide), 1) <= lax.broadcasted_iota(
        jnp.int32, (bands, wide), 0)
    w_ref[...] = jnp.where(keep, m[...], 0.0)[:, :bands]


def inverse_call(packed, bands, count):
    wide = -(-bands // LANES) * LANES
    return pl.pallas_call(
        functools.partial(inverse_kernel, bands, count),
        out_shape=jax.ShapeDtypeStruct((bands, bands), jnp.float32),
        in_specs=[pl.BlockSpec(memory_space=pltpu.VMEM)],
        out_specs=pl.BlockSpec(memory_space=pltpu.VMEM),
        scratch_shapes=[pltpu.VMEM((bands, wide), jnp.float32)],
    )(packed)

BANDS = 432
LD = 32
SD = 16


alpha_lift = -1.586134342059924
beta_lift = -0.052980118572961
gamma_lift = 0.882911075530934
delta_lift = 0.443506852043971
scale_lift = 1.230174104914001


def passed_along(array, axis, by):
    count = lax.axis_size(axis)
    pairs = [(i, i + by) for i in range(count) if 0 <= i + by < count]
    return lax.ppermute(array, axis, pairs)


def with_halo(block, sides, width):
    for axis, dim in sides:
        count = lax.axis_size(axis)
        forward = [(i, i + 1) for i in range(count - 1)]
        backward = [(target, source) for source, target in forward]
        low = lax.ppermute(
            lax.slice_in_dim(block, block.shape[dim] - width, None, axis=dim), axis, forward
        )
        high = lax.ppermute(lax.slice_in_dim(block, 0, width, axis=dim), axis, backward)
        block = jnp.concatenate([low, block, high], axis=dim)
    return block


def lines_next(edge):
    return passed_along(edge, "line", -1)


def lines_prev(edge):
    return passed_along(edge, "line", 1)


def split_pairs(values, axis):
    length = values.shape[axis]
    return (
        lax.slice_in_dim(values, 0, length, 2, axis),
        lax.slice_in_dim(values, 1, length, 2, axis),
    )


def lift_steps(values, axis, fetch_next, fetch_prev, at_first, at_last):
    evens, odds = split_pairs(values, axis)
    half = evens.shape[axis]
    for weight_odd, weight_even in ((alpha_lift, beta_lift), (gamma_lift, delta_lift)):
        own_last = lax.slice_in_dim(evens, half - 1, half, 1, axis)
        arrived = fetch_next(lax.slice_in_dim(evens, 0, 1, 1, axis))
        beyond = jnp.where(at_last, own_last, arrived)
        following = jnp.concatenate([lax.slice_in_dim(evens, 1, half, 1, axis), beyond], axis)
        odds = odds + weight_odd * (evens + following)
        own_first = lax.slice_in_dim(odds, 0, 1, 1, axis)
        received = fetch_prev(lax.slice_in_dim(odds, half - 1, half, 1, axis))
        before = jnp.where(at_first, own_first, received)
        preceding = jnp.concatenate([before, lax.slice_in_dim(odds, 0, half - 1, 1, axis)], axis)
        evens = evens + weight_even * (preceding + odds)
    return (evens / scale_lift, odds * scale_lift)


def lift_rims(values, at_first, at_last):
    length = values.shape[2]
    widened = with_halo(values, (("samp", 2),), 4)
    from_left = widened[:, :, :4]
    from_right = widened[:, :, length + 4 :]
    with_right = jnp.concatenate([values, from_right], 2)
    with_left = jnp.concatenate([from_left, values], 2)
    left_mirror = jnp.flip(with_right[:, :, 1:5], axis=2)
    right_mirror = jnp.flip(with_left[:, :, length - 1 : length + 3], axis=2)
    left_rim = jnp.where(at_first, left_mirror, from_left)
    right_rim = jnp.where(at_last, right_mirror, from_right)
    extended = jnp.concatenate([left_rim, values, right_rim], 2)
    evens, odds = split_pairs(extended, 2)
    odds = odds[..., :-1] + alpha_lift * (evens[..., :-1] + evens[..., 1:])
    evens = evens[..., 1:-1] + beta_lift * (odds[..., :-1] + odds[..., 1:])
    odds = odds[..., 1:-1] + gamma_lift * (evens[..., :-1] + evens[..., 1:])
    evens = evens[..., 1:-1] + delta_lift * (odds[..., :-1] + odds[..., 1:])
    return (evens / scale_lift, odds[..., 1:] * scale_lift)


def local(cube):
    band_count = BANDS
    line_count = LD
    samples = SD
    tile = cube.reshape(band_count, line_count, samples)
    pixels = line_count * samples
    devices = lax.axis_size("samp") * lax.axis_size("line")
    centered, packed = gram_call(cube, band_count, pixels)
    whitener = inverse_call(packed, band_count, pixels * devices)
    components = jnp.dot(
        whitener, centered, precision=lax.Precision.HIGHEST, preferred_element_type=jnp.float32
    ).reshape(tile.shape)
    samp_first = lax.axis_index("samp") == 0
    samp_last = lax.axis_index("samp") == lax.axis_size("samp") - 1
    line_first = lax.axis_index("line") == 0
    line_last = lax.axis_index("line") == lax.axis_size("line") - 1

    def decompose(values):
        low_s, high_s = lift_rims(values, samp_first, samp_last)
        joined = jnp.concatenate([low_s, high_s], 2)
        low_l, high_l = lift_steps(joined, 1, lines_next, lines_prev, line_first, line_last)
        middle = low_s.shape[2]
        details = jnp.stack([high_l[:, :, :middle], low_l[:, :, middle:], high_l[:, :, middle:]])
        return (low_l[:, :, :middle], details)

    approx1, details1 = decompose(components)
    approx2, details2 = decompose(approx1)
    approx3, details3 = decompose(approx2)
    return (details1.reshape(-1), details2.reshape(-1), details3.reshape(-1), approx3.reshape(-1))


def solution(mesh):
    in_specs = (P(("groups", "samp", "line")),)
    out_specs = (
        P(("groups", "samp", "line")),
        P(("groups", "samp", "line")),
        P(("groups", "samp", "line")),
        P(("groups", "samp", "line")),
    )
    return jax.shard_map(local, mesh=mesh, in_specs=in_specs, out_specs=out_specs, check_vma=False)
```

```python
import functools
import jax
import jax.numpy as jnp
from jax import lax
from jax.experimental import pallas as pl
from jax.experimental.pallas import tpu as pltpu
from jax.sharding import PartitionSpec as P

BANDS = 432
LD = 32
SD = 16

MESH = pl.DeviceIdType.MESH
HIGH = lax.Precision.HIGHEST
LANES = 128


def blocks_of(bands):
    rows = [bands - start for start in range(0, bands, LANES)]
    offsets = [sum(rows[:i]) for i in range(len(rows))]
    return rows, offsets


alpha_lift = -1.586134342059924
beta_lift = -0.052980118572961
gamma_lift = 0.882911075530934
delta_lift = 0.443506852043971
scale_lift = 1.230174104914001
RIM = 4


def lift_list(values):
    evens, odds = values[0::2], values[1::2]
    odds = [o + alpha_lift * (e + f) for o, e, f in zip(odds[:-1], evens[:-1], evens[1:])]
    evens = [e + beta_lift * (o + q) for e, o, q in zip(evens[1:-1], odds[:-1], odds[1:])]
    odds = [o + gamma_lift * (e + f) for o, e, f in zip(odds[1:-1], evens[:-1], evens[1:])]
    evens = [e + delta_lift * (o + q) for e, o, q in zip(evens[1:-1], odds[:-1], odds[1:])]
    return [e * (1.0 / scale_lift) for e in evens], [o * scale_lift for o in odds[1:]]


def lift_lines(src, halo, dst, lines, width, ln):
    half = lines // 2
    for t in range(src.shape[0]):
        own = [src[t, i * width:(i + 1) * width] for i in range(lines)]
        got = [halo[t, i * width:(i + 1) * width] for i in range(RIM)]
        before = [jnp.where(ln == 0, own[RIM - i], got[i]) for i in range(RIM)]
        after = [jnp.where(ln == 0, got[i], own[lines - 2 - i]) for i in range(RIM)]
        low, high = lift_list(before + own + after)
        for i in range(half):
            dst[t, i * width:(i + 1) * width] = low[i]
            dst[t, (half + i) * width:(half + i + 1) * width] = high[i]


def rims(z, lines, width, left, right):
    for t in range(z.shape[0]):
        for c in range(RIM):
            left[t, c * lines:(c + 1) * lines] = z[t, pl.ds(c, lines, stride=width), :]
            right[t, c * lines:(c + 1) * lines] = z[t, pl.ds(width - RIM + c, lines, stride=width), :]


def lift_samples(z, from_left, from_right, lines, width, first, last, dests):
    half = lines // 2
    for t in range(z.shape[0]):
        own = [z[t, pl.ds(s, lines, stride=width), :] for s in range(width)]
        left = [from_left[t, c * lines:(c + 1) * lines] for c in range(RIM)]
        right = [from_right[t, c * lines:(c + 1) * lines] for c in range(RIM)]
        whole = left + own + right
        before = [jnp.where(first, whole[2 * RIM - i], left[i]) for i in range(RIM)]
        after = [jnp.where(last, whole[RIM + width - 2 - i], right[i]) for i in range(RIM)]
        low, high = lift_list(before + own + after)
        for i in range(width // 2):
            for (ref, base), value in zip(dests, (low[i][:half], low[i][half:], high[i][:half], high[i][half:])):
                ref[t, pl.ds(base + i, half, stride=width // 2), :] = value


def gram_kernel(samp, line, bands, lines, width, x_ref, t_ref, p_ref, v1, v2, v3, z1, z2, z3, n1, n2, n3, el1, er1, el2, er2, el3, er3, fl1, fr1, fl2, fr2, fl3, fr3,
                l_send, l_recv, r_send, r_recv, xs, sums, sums_in, g, half_in,
                chunk_in, tot, s_send, s_recv, h_send, h_recv, c_send, c_recv, a_send, a_recv,
                b_send, b_recv):
    me, ln = lax.axis_index("samp"), lax.axis_index("line")
    devices = samp * line
    pixels = lines * width
    first, last = me == 0, me == samp - 1
    flat = me * line + ln
    packs = pixels // LANES
    padded = xs.shape[0]

    def peer(d):
        other = lax.rem(flat + d, devices)
        return {"samp": other // line, "line": lax.rem(other, line)}

    def line_copy(level, src, dst, tall, wide):
        rows = RIM * wide
        start = pl.multiple_of((1 - ln) * ((tall - RIM) * wide), 8)
        copy = pltpu.make_async_remote_copy(src.at[:, pl.ds(start, rows)], dst, l_send.at[level], l_recv.at[level],
                                            device_id={"line": 1 - ln}, device_id_type=MESH)
        copy.start()
        return copy

    def rim_copies(level, left, right, from_left, from_right):
        below = pltpu.make_async_remote_copy(left, from_right, r_send.at[level, 0], r_recv.at[level, 0],
                                             device_id={"samp": jnp.maximum(me - 1, 0)}, device_id_type=MESH)
        above = pltpu.make_async_remote_copy(right, from_left, r_send.at[level, 1], r_recv.at[level, 1],
                                             device_id={"samp": jnp.minimum(me + 1, samp - 1)}, device_id_type=MESH)

        @pl.when(me > 0)
        def _():
            below.start()

        @pl.when(me < samp - 1)
        def _():
            above.start()

        return below, above

    def rim_wait(pair):
        below, above = pair

        @pl.when(me > 0)
        def _():
            below.wait_send()
            above.wait_recv()

        @pl.when(me < samp - 1)
        def _():
            above.wait_send()
            below.wait_recv()

    for ref in (fl1, fr1, fl2, fr2, fl3, fr3):
        ref[...] = jnp.zeros_like(ref)
    barrier = pltpu.get_barrier_semaphore()
    for d in range(1, devices):
        pl.semaphore_signal(barrier, inc=1, device_id=peer(d), device_id_type=MESH)
    if padded > bands:
        xs[bands:, :] = jnp.zeros((padded - bands, pixels), jnp.float32)
    for q in range(packs):
        xs[0:bands, q * LANES:(q + 1) * LANES] = x_ref[pl.ds(q, bands, stride=packs), :]
    sums[...] = lax.dot_general(jnp.ones((8, pixels), jnp.float32), xs[...], (((1,), (1,)), ((), ())),
                                precision=HIGH, preferred_element_type=jnp.float32)
    pl.semaphore_wait(barrier, devices - 1)
    copies = []
    for d in range(1, devices):
        copy = pltpu.make_async_remote_copy(sums, sums_in.at[d - 1], s_send.at[d - 1], s_recv.at[d - 1],
                                            device_id=peer(d), device_id_type=MESH)
        copy.start()
        copies.append(copy)
    for copy in copies:
        copy.wait()
    total = sums[...]
    for d in range(1, devices):
        total = total + sums_in[d - 1]
    mean = jnp.transpose(total / float(pixels * devices))[:, 0:1]
    xs[...] = xs[...] - mean
    for t in range(v1.shape[0]):
        v1[t] = jnp.transpose(xs[t * LANES:(t + 1) * LANES, :])
    lines1 = line_copy(0, v1, n1, lines, width)
    rows, offsets = blocks_of(bands)
    for q, (count, offset) in enumerate(zip(rows, offsets)):
        g[offset:offset + count, :] = lax.dot_general(
            xs[q * LANES:q * LANES + count, :], xs[q * LANES:(q + 1) * LANES, :],
            (((1,), (1,)), ((), ())), precision=HIGH, preferred_element_type=jnp.float32)
    used = offsets[-1] + rows[-1]
    if g.shape[0] > used:
        g[used:, :] = jnp.zeros((g.shape[0] - used, LANES), jnp.float32)
    half = g.shape[0] // line
    chunk = half // samp
    copies = []
    for d in range(1, line):
        other = lax.rem(ln + d, line)
        copy = pltpu.make_async_remote_copy(
            g.at[pl.ds(pl.multiple_of(other * half, 8), half)], half_in.at[d - 1], h_send.at[d - 1],
            h_recv.at[d - 1], device_id={"line": other}, device_id_type=MESH)
        copy.start()
        copies.append(copy)
    lines1.wait()
    lift_lines(v1, n1, z1, lines, width, ln)
    rims(z1, lines, width, el1, er1)
    for copy in copies:
        copy.wait()
    mine = pl.ds(pl.multiple_of(ln * half, 8), half)
    value = g[mine, :]
    for d in range(1, line):
        value = value + half_in[d - 1]
    g[mine, :] = value
    copies = []
    for d in range(1, samp):
        other = lax.rem(me + d, samp)
        copy = pltpu.make_async_remote_copy(
            g.at[pl.ds(pl.multiple_of(ln * half + other * chunk, 8), chunk)], chunk_in.at[d - 1],
            c_send.at[d - 1], c_recv.at[d - 1], device_id={"samp": other}, device_id_type=MESH)
        copy.start()
        copies.append(copy)
    pair = rim_copies(0, el1, er1, fl1, fr1)
    rim_wait(pair)
    h, w = lines // 2, width // 2
    one = h * w
    lift_samples(z1, fl1, fr1, lines, width, first, last, ((v2, 0), (t_ref, 0), (t_ref, one), (t_ref, 2 * one)))
    lines2 = line_copy(1, v2, n2, h, w)
    lines2.wait()
    lift_lines(v2, n2, z2, h, w, ln)
    rims(z2, h, w, el2, er2)
    pair2 = rim_copies(1, el2, er2, fl2, fr2)
    for copy in copies:
        copy.wait()
    own = pl.ds(pl.multiple_of(ln * half + me * chunk, 8), chunk)
    value = g[own, :]
    for d in range(1, samp):
        value = value + chunk_in[d - 1]
    tot[own, :] = value
    copies = []
    for d in range(1, samp):
        other = lax.rem(me + d, samp)
        copy = pltpu.make_async_remote_copy(tot.at[own], tot.at[own], a_send.at[d - 1], a_recv.at[d - 1],
                                            device_id={"samp": other}, device_id_type=MESH)
        copy.start()
        copies.append(copy)
    rim_wait(pair2)
    two, base2 = one // 4, 3 * one
    lift_samples(z2, fl2, fr2, h, w, first, last,
                 ((v3, 0), (t_ref, base2), (t_ref, base2 + two), (t_ref, base2 + 2 * two)))
    h, w = h // 2, w // 2
    lines3 = line_copy(2, v3, n3, h, w)
    lines3.wait()
    lift_lines(v3, n3, z3, h, w, ln)
    rims(z3, h, w, el3, er3)
    pair3 = rim_copies(2, el3, er3, fl3, fr3)
    for copy in copies:
        copy.wait()
    copies = []
    for d in range(1, line):
        other = lax.rem(ln + d, line)
        copy = pltpu.make_async_remote_copy(tot.at[mine], tot.at[mine], b_send.at[d - 1], b_recv.at[d - 1],
                                            device_id={"line": other}, device_id_type=MESH)
        copy.start()
        copies.append(copy)
    rim_wait(pair3)
    three, base3 = two // 4, base2 + 3 * two
    lift_samples(z3, fl3, fr3, h, w, first, last,
                 ((t_ref, base3 + 3 * three), (t_ref, base3), (t_ref, base3 + three), (t_ref, base3 + 2 * three)))
    for copy in copies:
        copy.wait()
    p_ref[...] = tot[...]


def gram_call(cube, bands, lines, width):
    pixels = lines * width
    samp, line = lax.axis_size("samp"), lax.axis_size("line")
    devices = samp * line
    rows, offsets = blocks_of(bands)
    used = offsets[-1] + rows[-1]
    unit = 8 * devices
    total = -(-used // unit) * unit
    padded = -(-bands // LANES) * LANES
    f32 = jnp.float32
    sem = pltpu.SemaphoreType.DMA
    return pl.pallas_call(
        functools.partial(gram_kernel, samp, line, bands, lines, width),
        out_shape=(jax.ShapeDtypeStruct((padded // LANES, pixels, LANES), f32), jax.ShapeDtypeStruct((total, LANES), f32)),
        in_specs=[pl.BlockSpec(memory_space=pltpu.VMEM)],
        out_specs=(pl.BlockSpec(memory_space=pltpu.VMEM), pl.BlockSpec(memory_space=pltpu.VMEM)),
        scratch_shapes=[
            *[pltpu.VMEM((padded // LANES, pixels // 4 ** i, LANES), f32) for i in (0, 1, 2)],
            *[pltpu.VMEM((padded // LANES, pixels // 4 ** i, LANES), f32) for i in (0, 1, 2)],
            *[pltpu.VMEM((padded // LANES, RIM * width // 2 ** i, LANES), f32) for i in (0, 1, 2)],
            *[pltpu.VMEM((padded // LANES, RIM * lines // 2 ** i, LANES), f32) for i in (0, 0, 1, 1, 2, 2)],
            *[pltpu.VMEM((padded // LANES, RIM * lines // 2 ** i, LANES), f32) for i in (0, 0, 1, 1, 2, 2)],
            sem((3,)), sem((3,)), sem((3, 2)), sem((3, 2)),
            pltpu.VMEM((padded, pixels), f32), pltpu.VMEM((8, padded), f32),
            pltpu.VMEM((devices - 1, 8, padded), f32), pltpu.VMEM((total, LANES), f32),
            pltpu.VMEM((line - 1, total // line, LANES), f32),
            pltpu.VMEM((samp - 1, total // devices, LANES), f32), pltpu.VMEM((total, LANES), f32),
            sem((devices - 1,)), sem((devices - 1,)), sem((line - 1,)), sem((line - 1,)),
            sem((samp - 1,)), sem((samp - 1,)), sem((samp - 1,)), sem((samp - 1,)),
            sem((line - 1,)), sem((line - 1,)),
        ],
        compiler_params=pltpu.CompilerParams(collective_id=0, has_side_effects=True),
    )(cube.reshape(-1, LANES))


def split3(value):
    first = value.astype(jnp.bfloat16).astype(jnp.float32)
    rest = value - first
    second = rest.astype(jnp.bfloat16).astype(jnp.float32)
    return first, second, rest - second


def inverse_kernel(bands, count, p_ref, t_ref, o1_ref, rest_ref, m):
    wide = m.shape[1]
    rows, offsets = blocks_of(bands)
    diag = lax.broadcasted_iota(jnp.int32, (LANES, LANES), 0) == lax.broadcasted_iota(
        jnp.int32, (LANES, LANES), 1)
    scale = 1.0 / float(count)
    trace = jnp.zeros((1, 1), jnp.float32)
    for q, offset in enumerate(offsets):
        size = min(LANES, rows[q])
        block = p_ref[offset:offset + size, :]
        kept = jnp.where(diag[:size], block, 0.0)
        trace = trace + jnp.sum(jnp.sum(kept, axis=0, keepdims=True), axis=1, keepdims=True)
    ridge = trace * scale * (0.01 / bands)
    for q, offset in enumerate(offsets):
        for b in range(q, len(rows)):
            size = min(LANES, rows[b])
            start = offset + (b - q) * LANES
            block = p_ref[start:start + size, :] * scale
            if b == q:
                low = jnp.where(diag[:size], block + ridge, block)
                m[q * LANES:q * LANES + size, q * LANES:(q + 1) * LANES] = low
            else:
                if size < LANES:
                    block = jnp.concatenate([block, jnp.zeros((LANES - size, LANES), jnp.float32)], axis=0)
                m[q * LANES:(q + 1) * LANES, b * LANES:(b + 1) * LANES] = jnp.transpose(block)
                m[b * LANES:b * LANES + size, q * LANES:(q + 1) * LANES] = block[:size]
    sub = lax.broadcasted_iota(jnp.int32, (8, LANES), 0)
    lane = lax.broadcasted_iota(jnp.int32, (8, LANES), 1)

    for c in range(len(rows)):
        top = c * LANES
        span = bands - top

        def step(j, carry):
            row = pl.multiple_of(top + 8 * j, 8)
            here = m[pl.ds(row, 8), top:top + LANES]
            small = pltpu.roll(here, lax.rem(LANES - 8 * j, LANES), 1)
            columns = [jnp.broadcast_to(small[:, b:b + 1], (8, LANES)) for b in range(8)]
            d = [[jnp.broadcast_to(columns[b][a:a + 1, :], (8, LANES)) if b <= a else None
                  for b in range(8)] for a in range(8)]
            low = [[None] * 8 for _ in range(8)]
            root = [None] * 8
            for b in range(8):
                root[b] = lax.rsqrt(d[b][b])
                for a in range(b + 1, 8):
                    low[a][b] = d[a][b] * root[b]
                for a in range(b + 1, 8):
                    for e in range(b + 1, a + 1):
                        d[a][e] = d[a][e] - low[a][b] * low[e][b]
            inv = [[None] * 8 for _ in range(8)]
            for b in range(8):
                inv[b][b] = root[b]
                for a in range(b + 1, 8):
                    acc = low[a][b] * inv[b][b]
                    for e in range(b + 1, a):
                        acc = acc + low[a][e] * inv[e][b]
                    inv[a][b] = -(acc * root[a])
            wcol = []
            for b in range(8):
                col = jnp.where(sub == b, inv[b][b], 0.0)
                for a in range(b + 1, 8):
                    col = jnp.where(sub == a, inv[a][b], col)
                wcol.append(col)
            tiles = []
            for t in range(wide // LANES):
                acc = None
                panel = m[pl.ds(row, 8), t * LANES:(t + 1) * LANES]
                for b in range(8):
                    term = wcol[b] * panel[b:b + 1, :]
                    acc = term if acc is None else acc + term
                if t == c:
                    for b in range(8):
                        acc = jnp.where(lane == 8 * j + b, wcol[b], acc)
                tiles.append(acc)
            r = jnp.concatenate(tiles, axis=1)
            m[pl.ds(row, 8), :] = r
            one, two, three = split3(r)
            right = jnp.concatenate([one, two, three, one, two, one], axis=0)
            cols = lax.broadcasted_iota(jnp.int32, (8, wide), 1)
            keep = (cols >= row + 8).astype(jnp.float32)
            l1, l2, l3 = one * keep, two * keep, three * keep
            left = jnp.concatenate([l1, l1, l1, l2, l2, l3], axis=0)[:, top:]
            update = lax.dot_general(
                jnp.transpose(left).astype(jnp.bfloat16), right.astype(jnp.bfloat16),
                (((1,), (0,)), ((), ())), preferred_element_type=jnp.float32)
            for t in range(wide // LANES):
                part = slice(t * LANES, (t + 1) * LANES)
                old = m[top:bands, part]
                if t == c:
                    line_ids = lax.broadcasted_iota(jnp.int32, (span, LANES), 0)
                    lane_ids = lax.broadcasted_iota(jnp.int32, (span, LANES), 1)
                    inside = (lane_ids >= 8 * j) & (lane_ids < 8 * j + 8) & (line_ids >= 8 * j + 8)
                    old = jnp.where(inside, 0.0, old)
                m[top:bands, part] = old - update[:span, part]
            return carry

        lax.fori_loop(0, min(LANES, span) // 8, step, 0)
    keep = lax.broadcasted_iota(jnp.int32, (bands, wide), 1) <= lax.broadcasted_iota(
        jnp.int32, (bands, wide), 0)
    m[...] = jnp.where(keep, m[...], 0.0)
    for q in range(t_ref.shape[1] // LANES):
        part = jnp.concatenate([t_ref[t, q * LANES:(q + 1) * LANES, :] for t in range(wide // LANES)], axis=1)
        out = lax.dot_general(m[...], part, (((1,), (1,)), ((), ())),
                              precision=HIGH, preferred_element_type=jnp.float32)
        if q < o1_ref.shape[0]:
            o1_ref[q] = out
        else:
            rest_ref[...] = out


def inverse_call(packed, coefs, bands, count):
    wide = -(-bands // LANES) * LANES
    f32 = jnp.float32
    vmem = pl.BlockSpec(memory_space=pltpu.VMEM)
    return pl.pallas_call(
        functools.partial(inverse_kernel, bands, count),
        out_shape=(jax.ShapeDtypeStruct((3, bands, LANES), f32), jax.ShapeDtypeStruct((bands, LANES), f32)),
        in_specs=[vmem, vmem],
        out_specs=(vmem, vmem),
        scratch_shapes=[pltpu.VMEM((bands, wide), f32)],
    )(packed, coefs)


def local(cube):
    pixels = LD * SD
    devices = lax.axis_size("samp") * lax.axis_size("line")
    coefs, packed = gram_call(cube, BANDS, LD, SD)
    first, rest = inverse_call(packed, coefs, BANDS, pixels * devices)
    second = pixels // 16
    third = second // 4
    level2 = [rest[:, i * second:(i + 1) * second] for i in range(3)]
    base = 3 * second
    level3 = [rest[:, base + i * third:base + (i + 1) * third] for i in range(3)]
    approx = rest[:, base + 3 * third:base + 4 * third]
    return (first.reshape(-1), jnp.stack(level2).reshape(-1), jnp.stack(level3).reshape(-1), approx.reshape(-1))


def solution(mesh):
    in_specs = (P(("groups", "samp", "line")),)
    out_specs = (
        P(("groups", "samp", "line")),
        P(("groups", "samp", "line")),
        P(("groups", "samp", "line")),
        P(("groups", "samp", "line")),
    )
    return jax.shard_map(local, mesh=mesh, in_specs=in_specs, out_specs=out_specs, check_vma=False)
```

```python
import functools
import jax
import jax.numpy as jnp
from jax import lax
from jax.experimental import pallas as pl
from jax.experimental.pallas import tpu as pltpu
from jax.sharding import PartitionSpec as P

BANDS = 432
LD = 32
SD = 16

MESH = pl.DeviceIdType.MESH
HIGH = lax.Precision.HIGHEST
LANES = 128


def blocks_of(bands):
    rows = [bands - start for start in range(0, bands, LANES)]
    offsets = [sum(rows[:i]) for i in range(len(rows))]
    return rows, offsets


alpha_lift = -1.586134342059924
beta_lift = -0.052980118572961
gamma_lift = 0.882911075530934
delta_lift = 0.443506852043971
scale_lift = 1.230174104914001
RIM = 4


def lift_list(values):
    evens, odds = values[0::2], values[1::2]
    odds = [o + alpha_lift * (e + f) for o, e, f in zip(odds[:-1], evens[:-1], evens[1:])]
    evens = [e + beta_lift * (o + q) for e, o, q in zip(evens[1:-1], odds[:-1], odds[1:])]
    odds = [o + gamma_lift * (e + f) for o, e, f in zip(odds[1:-1], evens[:-1], evens[1:])]
    evens = [e + delta_lift * (o + q) for e, o, q in zip(evens[1:-1], odds[:-1], odds[1:])]
    return [e * (1.0 / scale_lift) for e in evens], [o * scale_lift for o in odds[1:]]


def lift_lines(src, halo, dst, lines, width, ln):
    half = lines // 2
    for t in range(src.shape[0]):
        own = [src[t, i * width:(i + 1) * width] for i in range(lines)]
        got = [halo[t, i * width:(i + 1) * width] for i in range(RIM)]
        before = [jnp.where(ln == 0, own[RIM - i], got[i]) for i in range(RIM)]
        after = [jnp.where(ln == 0, got[i], own[lines - 2 - i]) for i in range(RIM)]
        low, high = lift_list(before + own + after)
        for i in range(half):
            dst[t, i * width:(i + 1) * width] = low[i]
            dst[t, (half + i) * width:(half + i + 1) * width] = high[i]


def rims(z, lines, width, left, right):
    for t in range(z.shape[0]):
        for c in range(RIM):
            left[t, c * lines:(c + 1) * lines] = z[t, pl.ds(c, lines, stride=width), :]
            right[t, c * lines:(c + 1) * lines] = z[t, pl.ds(width - RIM + c, lines, stride=width), :]


def lift_samples(z, from_left, from_right, lines, width, first, last, dests):
    half = lines // 2
    for t in range(z.shape[0]):
        own = [z[t, pl.ds(s, lines, stride=width), :] for s in range(width)]
        left = [from_left[t, c * lines:(c + 1) * lines] for c in range(RIM)]
        right = [from_right[t, c * lines:(c + 1) * lines] for c in range(RIM)]
        whole = left + own + right
        before = [jnp.where(first, whole[2 * RIM - i], left[i]) for i in range(RIM)]
        after = [jnp.where(last, whole[RIM + width - 2 - i], right[i]) for i in range(RIM)]
        low, high = lift_list(before + own + after)
        for i in range(width // 2):
            for (ref, base), value in zip(dests, (low[i][:half], low[i][half:], high[i][:half], high[i][half:])):
                ref[t, pl.ds(base + i, half, stride=width // 2), :] = value


def split3(value):
    first = value.astype(jnp.bfloat16).astype(jnp.float32)
    rest = value - first
    second = rest.astype(jnp.bfloat16).astype(jnp.float32)
    return first, second, rest - second


def gram_kernel(samp, line, bands, lines, width, x_ref, o1_ref, o2_ref, o3_ref, o4_ref, t_ref, m, rest, v1, v2, v3, z1, z2, z3, n1, n2, n3, el1, er1, el2, er2, el3, er3, fl1, fr1, fl2, fr2, fl3, fr3,
                l_send, l_recv, r_send, r_recv, xs, sums, sums_in, g, half_in,
                chunk_in, tot, s_send, s_recv, h_send, h_recv, c_send, c_recv, a_send, a_recv,
                b_send, b_recv):
    me, ln = lax.axis_index("samp"), lax.axis_index("line")
    devices = samp * line
    pixels = lines * width
    first, last = me == 0, me == samp - 1
    flat = me * line + ln
    packs = pixels // LANES
    padded = xs.shape[0]

    def peer(d):
        other = lax.rem(flat + d, devices)
        return {"samp": other // line, "line": lax.rem(other, line)}

    def line_copy(level, src, dst, tall, wide):
        rows = RIM * wide
        start = pl.multiple_of((1 - ln) * ((tall - RIM) * wide), 8)
        copy = pltpu.make_async_remote_copy(src.at[:, pl.ds(start, rows)], dst, l_send.at[level], l_recv.at[level],
                                            device_id={"line": 1 - ln}, device_id_type=MESH)
        copy.start()
        return copy

    def rim_copies(level, left, right, from_left, from_right):
        below = pltpu.make_async_remote_copy(left, from_right, r_send.at[level, 0], r_recv.at[level, 0],
                                             device_id={"samp": jnp.maximum(me - 1, 0)}, device_id_type=MESH)
        above = pltpu.make_async_remote_copy(right, from_left, r_send.at[level, 1], r_recv.at[level, 1],
                                             device_id={"samp": jnp.minimum(me + 1, samp - 1)}, device_id_type=MESH)

        @pl.when(me > 0)
        def _():
            below.start()

        @pl.when(me < samp - 1)
        def _():
            above.start()

        return below, above

    def rim_wait(pair):
        below, above = pair

        @pl.when(me > 0)
        def _():
            below.wait_send()
            above.wait_recv()

        @pl.when(me < samp - 1)
        def _():
            above.wait_send()
            below.wait_recv()

    for ref in (fl1, fr1, fl2, fr2, fl3, fr3):
        ref[...] = jnp.zeros_like(ref)
    barrier = pltpu.get_barrier_semaphore()
    for d in range(1, devices):
        pl.semaphore_signal(barrier, inc=1, device_id=peer(d), device_id_type=MESH)
    if padded > bands:
        xs[bands:, :] = jnp.zeros((padded - bands, pixels), jnp.float32)
    for q in range(packs):
        xs[0:bands, q * LANES:(q + 1) * LANES] = x_ref[pl.ds(q, bands, stride=packs), :]
    sums[...] = lax.dot_general(jnp.ones((8, pixels), jnp.float32), xs[...], (((1,), (1,)), ((), ())),
                                precision=HIGH, preferred_element_type=jnp.float32)[0:1]
    pl.semaphore_wait(barrier, devices - 1)
    copies = []
    for d in range(1, devices):
        copy = pltpu.make_async_remote_copy(sums, sums_in.at[d - 1], s_send.at[d - 1], s_recv.at[d - 1],
                                            device_id=peer(d), device_id_type=MESH)
        copy.start()
        copies.append(copy)
    for copy in copies:
        copy.wait()
    total = sums[...]
    for d in range(1, devices):
        total = total + sums_in[d - 1]
    mean = jnp.transpose(jnp.broadcast_to(total / float(pixels * devices), (8, padded)))[:, 0:1]
    xs[...] = xs[...] - mean
    rows, offsets = blocks_of(bands)
    for q, (count, offset) in enumerate(zip(rows, offsets)):
        g[offset:offset + count, :] = lax.dot_general(
            xs[q * LANES:q * LANES + count, :], xs[q * LANES:(q + 1) * LANES, :],
            (((1,), (1,)), ((), ())), precision=HIGH, preferred_element_type=jnp.float32)
    used = offsets[-1] + rows[-1]
    if g.shape[0] > used:
        g[used:, :] = jnp.zeros((g.shape[0] - used, LANES), jnp.float32)
    half = g.shape[0] // line
    chunk = half // samp
    copies = []
    for d in range(1, line):
        other = lax.rem(ln + d, line)
        copy = pltpu.make_async_remote_copy(
            g.at[pl.ds(pl.multiple_of(other * half, 8), half)], half_in.at[d - 1], h_send.at[d - 1],
            h_recv.at[d - 1], device_id={"line": other}, device_id_type=MESH)
        copy.start()
        copies.append(copy)
    for t in range(v1.shape[0]):
        v1[t] = jnp.transpose(xs[t * LANES:(t + 1) * LANES, :])
    lines1 = line_copy(0, v1, n1, lines, width)
    for copy in copies:
        copy.wait()
    mine = pl.ds(pl.multiple_of(ln * half, 8), half)
    value = g[mine, :]
    for d in range(1, line):
        value = value + half_in[d - 1]
    g[mine, :] = value
    copies = []
    for d in range(1, samp):
        other = lax.rem(me + d, samp)
        copy = pltpu.make_async_remote_copy(
            g.at[pl.ds(pl.multiple_of(ln * half + other * chunk, 8), chunk)], chunk_in.at[d - 1],
            c_send.at[d - 1], c_recv.at[d - 1], device_id={"samp": other}, device_id_type=MESH)
        copy.start()
        copies.append(copy)
    lines1.wait()
    lift_lines(v1, n1, z1, lines, width, ln)
    rims(z1, lines, width, el1, er1)
    for copy in copies:
        copy.wait()
    own = pl.ds(pl.multiple_of(ln * half + me * chunk, 8), chunk)
    value = g[own, :]
    for d in range(1, samp):
        value = value + chunk_in[d - 1]
    tot[own, :] = value
    copies = []
    for d in range(1, samp):
        other = lax.rem(me + d, samp)
        copy = pltpu.make_async_remote_copy(tot.at[own], tot.at[own], a_send.at[d - 1], a_recv.at[d - 1],
                                            device_id={"samp": other}, device_id_type=MESH)
        copy.start()
        copies.append(copy)
    pair = rim_copies(0, el1, er1, fl1, fr1)
    for copy in copies:
        copy.wait()
    copies = []
    for d in range(1, line):
        other = lax.rem(ln + d, line)
        copy = pltpu.make_async_remote_copy(tot.at[mine], tot.at[mine], b_send.at[d - 1], b_recv.at[d - 1],
                                            device_id={"line": other}, device_id_type=MESH)
        copy.start()
        copies.append(copy)
    for copy in copies:
        copy.wait()
    wide = m.shape[1]
    rows, offsets = blocks_of(bands)
    diag = lax.broadcasted_iota(jnp.int32, (LANES, LANES), 0) == lax.broadcasted_iota(
        jnp.int32, (LANES, LANES), 1)
    scale = 1.0 / float(pixels * devices)
    trace = jnp.zeros((1, 1), jnp.float32)
    for q, offset in enumerate(offsets):
        size = min(LANES, rows[q])
        block = tot[offset:offset + size, :]
        kept = jnp.where(diag[:size], block, 0.0)
        trace = trace + jnp.sum(jnp.sum(kept, axis=0, keepdims=True), axis=1, keepdims=True)
    ridge = trace * scale * (0.01 / bands)
    for q, offset in enumerate(offsets):
        for b in range(q, len(rows)):
            size = min(LANES, rows[b])
            start = offset + (b - q) * LANES
            block = tot[start:start + size, :] * scale
            if b == q:
                low = jnp.where(diag[:size], block + ridge, block)
                m[q * LANES:q * LANES + size, q * LANES:(q + 1) * LANES] = low
            else:
                if size < LANES:
                    block = jnp.concatenate([block, jnp.zeros((LANES - size, LANES), jnp.float32)], axis=0)
                m[q * LANES:(q + 1) * LANES, b * LANES:(b + 1) * LANES] = jnp.transpose(block)
                m[b * LANES:b * LANES + size, q * LANES:(q + 1) * LANES] = block[:size]
    sub = lax.broadcasted_iota(jnp.int32, (8, LANES), 0)
    lane = lax.broadcasted_iota(jnp.int32, (8, LANES), 1)

    def eliminate(c):
        top = c * LANES
        span = bands - top

        def step(j, carry):
            row = pl.multiple_of(top + 8 * j, 8)
            here = m[pl.ds(row, 8), top:top + LANES]
            small = pltpu.roll(here, lax.rem(LANES - 8 * j, LANES), 1)
            columns = [jnp.broadcast_to(small[:, b:b + 1], (8, LANES)) for b in range(8)]
            d = [[jnp.broadcast_to(columns[b][a:a + 1, :], (8, LANES)) if b <= a else None
                  for b in range(8)] for a in range(8)]
            low = [[None] * 8 for _ in range(8)]
            root = [None] * 8
            for b in range(8):
                root[b] = lax.rsqrt(d[b][b])
                for a in range(b + 1, 8):
                    low[a][b] = d[a][b] * root[b]
                for a in range(b + 1, 8):
                    for e in range(b + 1, a + 1):
                        d[a][e] = d[a][e] - low[a][b] * low[e][b]
            inv = [[None] * 8 for _ in range(8)]
            for b in range(8):
                inv[b][b] = root[b]
                for a in range(b + 1, 8):
                    acc = low[a][b] * inv[b][b]
                    for e in range(b + 1, a):
                        acc = acc + low[a][e] * inv[e][b]
                    inv[a][b] = -(acc * root[a])
            wcol = []
            for b in range(8):
                col = jnp.where(sub == b, inv[b][b], 0.0)
                for a in range(b + 1, 8):
                    col = jnp.where(sub == a, inv[a][b], col)
                wcol.append(col)
            tiles = []
            for t in range(wide // LANES):
                acc = None
                panel = m[pl.ds(row, 8), t * LANES:(t + 1) * LANES]
                for b in range(8):
                    term = wcol[b] * panel[b:b + 1, :]
                    acc = term if acc is None else acc + term
                if t == c:
                    for b in range(8):
                        acc = jnp.where(lane == 8 * j + b, wcol[b], acc)
                tiles.append(acc)
            r = jnp.concatenate(tiles, axis=1)
            m[pl.ds(row, 8), :] = r
            one, two, three = split3(r)
            right = jnp.concatenate([one, two, three, one, two, one], axis=0)
            cols = lax.broadcasted_iota(jnp.int32, (8, wide), 1)
            keep = (cols >= row + 8).astype(jnp.float32)
            l1, l2, l3 = one * keep, two * keep, three * keep
            left = jnp.concatenate([l1, l1, l1, l2, l2, l3], axis=0)[:, top:]
            update = lax.dot_general(
                jnp.transpose(left).astype(jnp.bfloat16), right.astype(jnp.bfloat16),
                (((1,), (0,)), ((), ())), preferred_element_type=jnp.float32)
            for t in range(wide // LANES):
                part = slice(t * LANES, (t + 1) * LANES)
                old = m[top:bands, part]
                if t == c:
                    line_ids = lax.broadcasted_iota(jnp.int32, (span, LANES), 0)
                    lane_ids = lax.broadcasted_iota(jnp.int32, (span, LANES), 1)
                    inside = (lane_ids >= 8 * j) & (lane_ids < 8 * j + 8) & (line_ids >= 8 * j + 8)
                    old = jnp.where(inside, 0.0, old)
                m[top:bands, part] = old - update[:span, part]
            return carry

        lax.fori_loop(0, min(LANES, span) // 8, step, 0)
    eliminate(0)
    rim_wait(pair)
    h, w = lines // 2, width // 2
    one = h * w
    lift_samples(z1, fl1, fr1, lines, width, first, last, ((v2, 0), (t_ref, 0), (t_ref, one), (t_ref, 2 * one)))
    lines2 = line_copy(1, v2, n2, h, w)
    eliminate(1)
    lines2.wait()
    lift_lines(v2, n2, z2, h, w, ln)
    rims(z2, h, w, el2, er2)
    pair2 = rim_copies(1, el2, er2, fl2, fr2)
    eliminate(2)
    rim_wait(pair2)
    two, base2 = one // 4, 3 * one
    lift_samples(z2, fl2, fr2, h, w, first, last,
                 ((v3, 0), (t_ref, base2), (t_ref, base2 + two), (t_ref, base2 + 2 * two)))
    h, w = h // 2, w // 2
    lines3 = line_copy(2, v3, n3, h, w)
    lines3.wait()
    lift_lines(v3, n3, z3, h, w, ln)
    rims(z3, h, w, el3, er3)
    pair3 = rim_copies(2, el3, er3, fl3, fr3)
    for c in range(3, len(rows)):
        eliminate(c)
    rim_wait(pair3)
    three, base3 = two // 4, base2 + 3 * two
    lift_samples(z3, fl3, fr3, h, w, first, last,
                 ((t_ref, base3 + 3 * three), (t_ref, base3), (t_ref, base3 + three), (t_ref, base3 + 2 * three)))
    keep = lax.broadcasted_iota(jnp.int32, (bands, wide), 1) <= lax.broadcasted_iota(
        jnp.int32, (bands, wide), 0)
    m[...] = jnp.where(keep, m[...], 0.0)
    for q in range(t_ref.shape[1] // LANES):
        part = jnp.concatenate([t_ref[t, q * LANES:(q + 1) * LANES, :] for t in range(wide // LANES)], axis=1)
        out = lax.dot_general(m[...], part, (((1,), (1,)), ((), ())),
                              precision=HIGH, preferred_element_type=jnp.float32)
        if q < o1_ref.shape[0]:
            o1_ref[q] = out
        else:
            rest[...] = out


    def pack(dest, at, lane0, wide_out):
        group = LANES // wide_out
        count = bands // group
        pieces = [rest[pl.ds(b, count, stride=group), :][:, lane0:lane0 + wide_out] for b in range(group)]
        dest[at:at + count, :] = jnp.concatenate(pieces, axis=1)

    for i in range(3):
        pack(o2_ref, i * (o2_ref.shape[0] // 3), i * two, two)
        pack(o3_ref, i * (o3_ref.shape[0] // 3), 3 * two + i * three, three)
    pack(o4_ref, 0, 3 * two + 3 * three, three)


def gram_call(cube, bands, lines, width):
    pixels = lines * width
    samp, line = lax.axis_size("samp"), lax.axis_size("line")
    devices = samp * line
    rows, offsets = blocks_of(bands)
    used = offsets[-1] + rows[-1]
    unit = 8 * devices
    total = -(-used // unit) * unit
    padded = -(-bands // LANES) * LANES
    f32 = jnp.float32
    sem = pltpu.SemaphoreType.DMA
    return pl.pallas_call(
        functools.partial(gram_kernel, samp, line, bands, lines, width),
        out_shape=(jax.ShapeDtypeStruct((3, bands, LANES), f32),
                   jax.ShapeDtypeStruct((3 * bands * (pixels // 16) // LANES, LANES), f32),
                   jax.ShapeDtypeStruct((3 * bands * (pixels // 64) // LANES, LANES), f32),
                   jax.ShapeDtypeStruct((bands * (pixels // 64) // LANES, LANES), f32)),
        in_specs=[pl.BlockSpec(memory_space=pltpu.VMEM)],
        out_specs=(pl.BlockSpec(memory_space=pltpu.VMEM),) * 4,
        scratch_shapes=[
            pltpu.VMEM((padded // LANES, pixels, LANES), f32), pltpu.VMEM((bands, padded), f32),
            pltpu.VMEM((bands, LANES), f32),
            *[pltpu.VMEM((padded // LANES, pixels // 4 ** i, LANES), f32) for i in (0, 1, 2)],
            *[pltpu.VMEM((padded // LANES, pixels // 4 ** i, LANES), f32) for i in (0, 1, 2)],
            *[pltpu.VMEM((padded // LANES, RIM * width // 2 ** i, LANES), f32) for i in (0, 1, 2)],
            *[pltpu.VMEM((padded // LANES, RIM * lines // 2 ** i, LANES), f32) for i in (0, 0, 1, 1, 2, 2)],
            *[pltpu.VMEM((padded // LANES, RIM * lines // 2 ** i, LANES), f32) for i in (0, 0, 1, 1, 2, 2)],
            sem((3,)), sem((3,)), sem((3, 2)), sem((3, 2)),
            pltpu.VMEM((padded, pixels), f32), pltpu.VMEM((1, padded), f32),
            pltpu.VMEM((devices - 1, 1, padded), f32), pltpu.VMEM((total, LANES), f32),
            pltpu.VMEM((line - 1, total // line, LANES), f32),
            pltpu.VMEM((samp - 1, total // devices, LANES), f32), pltpu.VMEM((total, LANES), f32),
            sem((devices - 1,)), sem((devices - 1,)), sem((line - 1,)), sem((line - 1,)),
            sem((samp - 1,)), sem((samp - 1,)), sem((samp - 1,)), sem((samp - 1,)),
            sem((line - 1,)), sem((line - 1,)),
        ],
        compiler_params=pltpu.CompilerParams(collective_id=0, has_side_effects=True),
    )(cube.reshape(-1, LANES))


def local(cube):
    return tuple(out.reshape(-1) for out in gram_call(cube, BANDS, LD, SD))


def solution(mesh):
    in_specs = (P(("groups", "samp", "line")),)
    out_specs = (
        P(("groups", "samp", "line")),
        P(("groups", "samp", "line")),
        P(("groups", "samp", "line")),
        P(("groups", "samp", "line")),
    )
    return jax.shard_map(local, mesh=mesh, in_specs=in_specs, out_specs=out_specs, check_vma=False)
```

```python
import functools
import jax
import jax.numpy as jnp
from jax import lax
from jax.experimental import pallas as pl
from jax.experimental.pallas import tpu as pltpu
from jax.sharding import PartitionSpec as P

BANDS = 432
LD = 32
SD = 16

MESH = pl.DeviceIdType.MESH
HIGH = lax.Precision.HIGHEST
LANES = 128


def blocks_of(bands):
    rows = [bands - start for start in range(0, bands, LANES)]
    offsets = [sum(rows[:i]) for i in range(len(rows))]
    return rows, offsets


alpha_lift = -1.586134342059924
beta_lift = -0.052980118572961
gamma_lift = 0.882911075530934
delta_lift = 0.443506852043971
scale_lift = 1.230174104914001
RIM = 4


def lift_list(values):
    evens, odds = values[0::2], values[1::2]
    odds = [o + alpha_lift * (e + f) for o, e, f in zip(odds[:-1], evens[:-1], evens[1:])]
    evens = [e + beta_lift * (o + q) for e, o, q in zip(evens[1:-1], odds[:-1], odds[1:])]
    odds = [o + gamma_lift * (e + f) for o, e, f in zip(odds[1:-1], evens[:-1], evens[1:])]
    evens = [e + delta_lift * (o + q) for e, o, q in zip(evens[1:-1], odds[:-1], odds[1:])]
    return [e * (1.0 / scale_lift) for e in evens], [o * scale_lift for o in odds[1:]]


def lift_lines(src, halo, dst, lines, width, ln):
    half = lines // 2
    for t in range(src.shape[0]):
        own = [src[t, i * width:(i + 1) * width] for i in range(lines)]
        got = [halo[t, i * width:(i + 1) * width] for i in range(RIM)]
        before = [jnp.where(ln == 0, own[RIM - i], got[i]) for i in range(RIM)]
        after = [jnp.where(ln == 0, got[i], own[lines - 2 - i]) for i in range(RIM)]
        low, high = lift_list(before + own + after)
        for i in range(half):
            dst[t, i * width:(i + 1) * width] = low[i]
            dst[t, (half + i) * width:(half + i + 1) * width] = high[i]


def rims(z, lines, width, left, right):
    for t in range(z.shape[0]):
        low = [z[t, pl.ds(s, lines, stride=width), :] for s in range(3)]
        top = [z[t, pl.ds(s, lines, stride=width), :] for s in range(width - 4, width)]
        left[t, :lines] = low[0]
        left[t, lines:] = low[0] + beta_lift * (low[1] + alpha_lift * (low[0] + low[2]))
        right[t, :lines] = top[3] + alpha_lift * top[2]
        right[t, lines:] = top[2] + beta_lift * (top[1] + alpha_lift * (top[0] + top[2]))


def lift_samples(z, from_left, from_right, lines, width, first, last, dests):
    half, n = lines // 2, width // 2
    for t in range(z.shape[0]):
        evens = [z[t, pl.ds(2 * i, lines, stride=width), :] for i in range(n)]
        odds = [z[t, pl.ds(2 * i + 1, lines, stride=width), :] for i in range(n)]
        beyond = jnp.where(last, evens[-1], from_right[t, :lines])
        odds1 = [o + alpha_lift * (e + f) for o, e, f in zip(odds, evens, evens[1:] + [beyond])]
        before = jnp.where(first, odds1[0], from_left[t, :lines] + alpha_lift * evens[0])
        evens1 = [e + beta_lift * (p + o) for e, p, o in zip(evens, [before] + odds1[:-1], odds1)]
        beyond = jnp.where(last, evens1[-1], from_right[t, lines:] + beta_lift * odds1[-1])
        odds2 = [o + gamma_lift * (e + f) for o, e, f in zip(odds1, evens1, evens1[1:] + [beyond])]
        outside = from_left[t, lines:] + beta_lift * before
        before = jnp.where(first, odds2[0], before + gamma_lift * (outside + evens1[0]))
        evens2 = [e + delta_lift * (p + o) for e, p, o in zip(evens1, [before] + odds2[:-1], odds2)]
        for i in range(n):
            low, high = evens2[i] * (1.0 / scale_lift), odds2[i] * scale_lift
            for (ref, base), value in zip(dests, (low[:half], low[half:], high[:half], high[half:])):
                ref[t, pl.ds(base + i, half, stride=n), :] = value


def split3(value):
    first = value.astype(jnp.bfloat16).astype(jnp.float32)
    rest = value - first
    second = rest.astype(jnp.bfloat16).astype(jnp.float32)
    return first, second, rest - second


def gram_kernel(samp, line, bands, lines, width, x_ref, o1_ref, o2_ref, o3_ref, o4_ref, t_ref, m, rest, corr, v1, v2, v3, z1, z2, z3, n1, n2, n3, el1, er1, el2, er2, el3, er3, fl1, fr1, fl2, fr2, fl3, fr3,
                l_send, l_recv, r_send, r_recv, xs, sums, sums_in, g, half_in,
                chunk_in, tot, s_send, s_recv, h_send, h_recv, c_send, c_recv, a_send, a_recv,
                b_send, b_recv):
    me, ln = lax.axis_index("samp"), lax.axis_index("line")
    devices = samp * line
    pixels = lines * width
    first, last = me == 0, me == samp - 1
    flat = me * line + ln
    packs = pixels // LANES
    padded = xs.shape[0]

    def peer(d):
        other = lax.rem(flat + d, devices)
        return {"samp": other // line, "line": lax.rem(other, line)}

    def line_copy(level, src, dst, tall, wide):
        rows = RIM * wide
        start = pl.multiple_of((1 - ln) * ((tall - RIM) * wide), 8)
        copy = pltpu.make_async_remote_copy(src.at[:, pl.ds(start, rows)], dst, l_send.at[level], l_recv.at[level],
                                            device_id={"line": 1 - ln}, device_id_type=MESH)
        copy.start()
        return copy

    def rim_copies(level, left, right, from_left, from_right):
        below = pltpu.make_async_remote_copy(left, from_right, r_send.at[level, 0], r_recv.at[level, 0],
                                             device_id={"samp": jnp.maximum(me - 1, 0)}, device_id_type=MESH)
        above = pltpu.make_async_remote_copy(right, from_left, r_send.at[level, 1], r_recv.at[level, 1],
                                             device_id={"samp": jnp.minimum(me + 1, samp - 1)}, device_id_type=MESH)

        @pl.when(me > 0)
        def _():
            below.start()

        @pl.when(me < samp - 1)
        def _():
            above.start()

        return below, above

    def rim_wait(pair):
        below, above = pair

        @pl.when(me > 0)
        def _():
            below.wait_send()
            above.wait_recv()

        @pl.when(me < samp - 1)
        def _():
            above.wait_send()
            below.wait_recv()

    for ref in (fl1, fr1, fl2, fr2, fl3, fr3):
        ref[...] = jnp.zeros_like(ref)
    barrier = pltpu.get_barrier_semaphore()
    for d in range(1, devices):
        pl.semaphore_signal(barrier, inc=1, device_id=peer(d), device_id_type=MESH)
    if padded > bands:
        xs[bands:, :] = jnp.zeros((padded - bands, pixels), jnp.float32)
    for q in range(packs):
        xs[0:bands, q * LANES:(q + 1) * LANES] = x_ref[pl.ds(q, bands, stride=packs), :]
    sums[...] = lax.dot_general(jnp.ones((8, pixels), jnp.float32), xs[...], (((1,), (1,)), ((), ())),
                                precision=HIGH, preferred_element_type=jnp.float32)[0:1]
    pl.semaphore_wait(barrier, devices - 1)
    copies = []
    for d in range(1, devices):
        copy = pltpu.make_async_remote_copy(sums, sums_in.at[d - 1], s_send.at[d - 1], s_recv.at[d - 1],
                                            device_id=peer(d), device_id_type=MESH)
        copy.start()
        copies.append(copy)
    sum_copies = copies
    local_mean = sums[...] / float(pixels)
    xs[...] = xs[...] - jnp.transpose(jnp.broadcast_to(local_mean, (8, padded)))[:, 0:1]
    rows, offsets = blocks_of(bands)
    for q, (count, offset) in enumerate(zip(rows, offsets)):
        g[offset:offset + count, :] = lax.dot_general(
            xs[q * LANES:q * LANES + count, :], xs[q * LANES:(q + 1) * LANES, :],
            (((1,), (1,)), ((), ())), precision=HIGH, preferred_element_type=jnp.float32)
    used = offsets[-1] + rows[-1]
    if g.shape[0] > used:
        g[used:, :] = jnp.zeros((g.shape[0] - used, LANES), jnp.float32)
    half = g.shape[0] // line
    chunk = half // samp
    copies = []
    for d in range(1, line):
        other = lax.rem(ln + d, line)
        copy = pltpu.make_async_remote_copy(
            g.at[pl.ds(pl.multiple_of(other * half, 8), half)], half_in.at[d - 1], h_send.at[d - 1],
            h_recv.at[d - 1], device_id={"line": other}, device_id_type=MESH)
        copy.start()
        copies.append(copy)
    for copy in copies:
        copy.wait()
    mine = pl.ds(pl.multiple_of(ln * half, 8), half)
    value = g[mine, :]
    for d in range(1, line):
        value = value + half_in[d - 1]
    g[mine, :] = value
    copies = []
    for d in range(1, samp):
        other = lax.rem(me + d, samp)
        copy = pltpu.make_async_remote_copy(
            g.at[pl.ds(pl.multiple_of(ln * half + other * chunk, 8), chunk)], chunk_in.at[d - 1],
            c_send.at[d - 1], c_recv.at[d - 1], device_id={"samp": other}, device_id_type=MESH)
        copy.start()
        copies.append(copy)
    for copy in sum_copies:
        copy.wait()
    total = sums[...]
    for d in range(1, devices):
        total = total + sums_in[d - 1]
    mean = total / float(pixels * devices)
    spread = jnp.concatenate([local_mean - mean] + [sums_in[d - 1] / float(pixels) - mean
                                                    for d in range(1, devices)], axis=0)
    shift = local_mean - mean
    for t in range(v1.shape[0]):
        v1[t] = jnp.transpose(xs[t * LANES:(t + 1) * LANES, :]) + shift[:, t * LANES:(t + 1) * LANES]
    lines1 = line_copy(0, v1, n1, lines, width)
    for q, (count, offset) in enumerate(zip(rows, offsets)):
        corr[offset:offset + count, :] = float(pixels) * lax.dot_general(
            spread, spread[:, q * LANES:(q + 1) * LANES], (((0,), (0,)), ((), ())), precision=HIGH,
            preferred_element_type=jnp.float32)[q * LANES:q * LANES + count]
    if g.shape[0] > used:
        corr[used:, :] = jnp.zeros((g.shape[0] - used, LANES), jnp.float32)
    lines1.wait()
    lift_lines(v1, n1, z1, lines, width, ln)
    rims(z1, lines, width, el1, er1)
    for copy in copies:
        copy.wait()
    own = pl.ds(pl.multiple_of(ln * half + me * chunk, 8), chunk)
    value = g[own, :] + corr[own, :]
    for d in range(1, samp):
        value = value + chunk_in[d - 1]
    tot[own, :] = value
    copies = []
    for d in range(1, samp):
        other = lax.rem(me + d, samp)
        copy = pltpu.make_async_remote_copy(tot.at[own], tot.at[own], a_send.at[d - 1], a_recv.at[d - 1],
                                            device_id={"samp": other}, device_id_type=MESH)
        copy.start()
        copies.append(copy)
    pair = rim_copies(0, el1, er1, fl1, fr1)
    for copy in copies:
        copy.wait()
    copies = []
    for d in range(1, line):
        other = lax.rem(ln + d, line)
        copy = pltpu.make_async_remote_copy(tot.at[mine], tot.at[mine], b_send.at[d - 1], b_recv.at[d - 1],
                                            device_id={"line": other}, device_id_type=MESH)
        copy.start()
        copies.append(copy)
    for copy in copies:
        copy.wait()
    wide = m.shape[1]
    rows, offsets = blocks_of(bands)
    diag = lax.broadcasted_iota(jnp.int32, (LANES, LANES), 0) == lax.broadcasted_iota(
        jnp.int32, (LANES, LANES), 1)
    scale = 1.0 / float(pixels * devices)
    trace = jnp.zeros((1, 1), jnp.float32)
    for q, offset in enumerate(offsets):
        size = min(LANES, rows[q])
        block = tot[offset:offset + size, :]
        kept = jnp.where(diag[:size], block, 0.0)
        trace = trace + jnp.sum(jnp.sum(kept, axis=0, keepdims=True), axis=1, keepdims=True)
    ridge = trace * scale * (0.01 / bands)
    for q, offset in enumerate(offsets):
        for b in range(q, len(rows)):
            size = min(LANES, rows[b])
            start = offset + (b - q) * LANES
            block = tot[start:start + size, :] * scale
            if b == q:
                low = jnp.where(diag[:size], block + ridge, block)
                m[q * LANES:q * LANES + size, q * LANES:(q + 1) * LANES] = low
            else:
                if size < LANES:
                    block = jnp.concatenate([block, jnp.zeros((LANES - size, LANES), jnp.float32)], axis=0)
                m[q * LANES:(q + 1) * LANES, b * LANES:(b + 1) * LANES] = jnp.transpose(block)
                m[b * LANES:b * LANES + size, q * LANES:(q + 1) * LANES] = block[:size]
    sub = lax.broadcasted_iota(jnp.int32, (8, LANES), 0)
    lane = lax.broadcasted_iota(jnp.int32, (8, LANES), 1)

    def eliminate(c):
        top = c * LANES
        span = bands - top

        def step(j, carry):
            row = pl.multiple_of(top + 8 * j, 8)
            here = m[pl.ds(row, 8), top:top + LANES]
            small = pltpu.roll(here, lax.rem(LANES - 8 * j, LANES), 1)
            columns = [jnp.broadcast_to(small[:, b:b + 1], (8, LANES)) for b in range(8)]
            d = [[jnp.broadcast_to(columns[b][a:a + 1, :], (8, LANES)) if b <= a else None
                  for b in range(8)] for a in range(8)]
            low = [[None] * 8 for _ in range(8)]
            root = [None] * 8
            for b in range(8):
                root[b] = lax.rsqrt(d[b][b])
                for a in range(b + 1, 8):
                    low[a][b] = d[a][b] * root[b]
                for a in range(b + 1, 8):
                    for e in range(b + 1, a + 1):
                        d[a][e] = d[a][e] - low[a][b] * low[e][b]
            inv = [[None] * 8 for _ in range(8)]
            for b in range(8):
                inv[b][b] = root[b]
                for a in range(b + 1, 8):
                    acc = low[a][b] * inv[b][b]
                    for e in range(b + 1, a):
                        acc = acc + low[a][e] * inv[e][b]
                    inv[a][b] = -(acc * root[a])
            wcol = []
            for b in range(8):
                col = jnp.where(sub == b, inv[b][b], 0.0)
                for a in range(b + 1, 8):
                    col = jnp.where(sub == a, inv[a][b], col)
                wcol.append(col)
            tiles = []
            for t in range(wide // LANES):
                acc = None
                panel = m[pl.ds(row, 8), t * LANES:(t + 1) * LANES]
                for b in range(8):
                    term = wcol[b] * panel[b:b + 1, :]
                    acc = term if acc is None else acc + term
                if t == c:
                    for b in range(8):
                        acc = jnp.where(lane == 8 * j + b, wcol[b], acc)
                tiles.append(acc)
            r = jnp.concatenate(tiles, axis=1)
            m[pl.ds(row, 8), :] = r
            one, two, three = split3(r)
            right = jnp.concatenate([one, two, three, one, two, one], axis=0)
            cols = lax.broadcasted_iota(jnp.int32, (8, wide), 1)
            keep = (cols >= row + 8).astype(jnp.float32)
            l1, l2, l3 = one * keep, two * keep, three * keep
            left = jnp.concatenate([l1, l1, l1, l2, l2, l3], axis=0)[:, top:]
            update = lax.dot_general(
                left.astype(jnp.bfloat16), right.astype(jnp.bfloat16),
                (((0,), (0,)), ((), ())), preferred_element_type=jnp.float32)
            for t in range(wide // LANES):
                part = slice(t * LANES, (t + 1) * LANES)
                old = m[top:bands, part]
                if t == c:
                    line_ids = lax.broadcasted_iota(jnp.int32, (span, LANES), 0)
                    lane_ids = lax.broadcasted_iota(jnp.int32, (span, LANES), 1)
                    inside = (lane_ids >= 8 * j) & (lane_ids < 8 * j + 8) & (line_ids >= 8 * j + 8)
                    old = jnp.where(inside, 0.0, old)
                m[top:bands, part] = old - update[:span, part]
            return carry

        lax.fori_loop(0, min(LANES, span) // 8, step, 0)
    eliminate(0)
    rim_wait(pair)
    h, w = lines // 2, width // 2
    one = h * w
    lift_samples(z1, fl1, fr1, lines, width, first, last, ((v2, 0), (t_ref, 0), (t_ref, one), (t_ref, 2 * one)))
    lines2 = line_copy(1, v2, n2, h, w)
    eliminate(1)
    lines2.wait()
    lift_lines(v2, n2, z2, h, w, ln)
    rims(z2, h, w, el2, er2)
    pair2 = rim_copies(1, el2, er2, fl2, fr2)
    eliminate(2)
    rim_wait(pair2)
    two, base2 = one // 4, 3 * one
    lift_samples(z2, fl2, fr2, h, w, first, last,
                 ((v3, 0), (t_ref, base2), (t_ref, base2 + two), (t_ref, base2 + 2 * two)))
    h, w = h // 2, w // 2
    lines3 = line_copy(2, v3, n3, h, w)
    lines3.wait()
    lift_lines(v3, n3, z3, h, w, ln)
    rims(z3, h, w, el3, er3)
    pair3 = rim_copies(2, el3, er3, fl3, fr3)
    for c in range(3, len(rows)):
        eliminate(c)
    rim_wait(pair3)
    three, base3 = two // 4, base2 + 3 * two
    lift_samples(z3, fl3, fr3, h, w, first, last,
                 ((t_ref, base3 + 3 * three), (t_ref, base3), (t_ref, base3 + three), (t_ref, base3 + 2 * three)))
    keep = lax.broadcasted_iota(jnp.int32, (bands, wide), 1) <= lax.broadcasted_iota(
        jnp.int32, (bands, wide), 0)
    m[...] = jnp.where(keep, m[...], 0.0)
    for q in range(t_ref.shape[1] // LANES):
        part = jnp.concatenate([t_ref[t, q * LANES:(q + 1) * LANES, :] for t in range(wide // LANES)], axis=1)
        out = lax.dot_general(m[...], part, (((1,), (1,)), ((), ())),
                              precision=HIGH, preferred_element_type=jnp.float32)
        if q < o1_ref.shape[0]:
            o1_ref[q] = out
        else:
            rest[...] = out


    def pack(dest, at, lane0, wide_out):
        group = LANES // wide_out
        count = bands // group
        pieces = [rest[pl.ds(b, count, stride=group), :][:, lane0:lane0 + wide_out] for b in range(group)]
        dest[at:at + count, :] = jnp.concatenate(pieces, axis=1)

    for i in range(3):
        pack(o2_ref, i * (o2_ref.shape[0] // 3), i * two, two)
        pack(o3_ref, i * (o3_ref.shape[0] // 3), 3 * two + i * three, three)
    pack(o4_ref, 0, 3 * two + 3 * three, three)


def gram_call(cube, bands, lines, width):
    pixels = lines * width
    samp, line = lax.axis_size("samp"), lax.axis_size("line")
    devices = samp * line
    rows, offsets = blocks_of(bands)
    used = offsets[-1] + rows[-1]
    unit = 8 * devices
    total = -(-used // unit) * unit
    padded = -(-bands // LANES) * LANES
    f32 = jnp.float32
    sem = pltpu.SemaphoreType.DMA
    return pl.pallas_call(
        functools.partial(gram_kernel, samp, line, bands, lines, width),
        out_shape=(jax.ShapeDtypeStruct((3, bands, LANES), f32),
                   jax.ShapeDtypeStruct((3 * bands * (pixels // 16) // LANES, LANES), f32),
                   jax.ShapeDtypeStruct((3 * bands * (pixels // 64) // LANES, LANES), f32),
                   jax.ShapeDtypeStruct((bands * (pixels // 64) // LANES, LANES), f32)),
        in_specs=[pl.BlockSpec(memory_space=pltpu.VMEM)],
        out_specs=(pl.BlockSpec(memory_space=pltpu.VMEM),) * 4,
        scratch_shapes=[
            pltpu.VMEM((padded // LANES, pixels, LANES), f32), pltpu.VMEM((bands, padded), f32),
            pltpu.VMEM((bands, LANES), f32), pltpu.VMEM((total, LANES), f32),
            *[pltpu.VMEM((padded // LANES, pixels // 4 ** i, LANES), f32) for i in (0, 1, 2)],
            *[pltpu.VMEM((padded // LANES, pixels // 4 ** i, LANES), f32) for i in (0, 1, 2)],
            *[pltpu.VMEM((padded // LANES, RIM * width // 2 ** i, LANES), f32) for i in (0, 1, 2)],
            *[pltpu.VMEM((padded // LANES, 2 * lines // 2 ** i, LANES), f32) for i in (0, 0, 1, 1, 2, 2)],
            *[pltpu.VMEM((padded // LANES, 2 * lines // 2 ** i, LANES), f32) for i in (0, 0, 1, 1, 2, 2)],
            sem((3,)), sem((3,)), sem((3, 2)), sem((3, 2)),
            pltpu.VMEM((padded, pixels), f32), pltpu.VMEM((1, padded), f32),
            pltpu.VMEM((devices - 1, 1, padded), f32), pltpu.VMEM((total, LANES), f32),
            pltpu.VMEM((line - 1, total // line, LANES), f32),
            pltpu.VMEM((samp - 1, total // devices, LANES), f32), pltpu.VMEM((total, LANES), f32),
            sem((devices - 1,)), sem((devices - 1,)), sem((line - 1,)), sem((line - 1,)),
            sem((samp - 1,)), sem((samp - 1,)), sem((samp - 1,)), sem((samp - 1,)),
            sem((line - 1,)), sem((line - 1,)),
        ],
        compiler_params=pltpu.CompilerParams(collective_id=0, has_side_effects=True),
    )(cube.reshape(-1, LANES))


def local(cube):
    return tuple(out.reshape(-1) for out in gram_call(cube, BANDS, LD, SD))


def solution(mesh):
    in_specs = (P(("groups", "samp", "line")),)
    out_specs = (
        P(("groups", "samp", "line")),
        P(("groups", "samp", "line")),
        P(("groups", "samp", "line")),
        P(("groups", "samp", "line")),
    )
    return jax.shard_map(local, mesh=mesh, in_specs=in_specs, out_specs=out_specs, check_vma=False)
```

```python
import functools
import jax
import jax.numpy as jnp
from jax import lax
from jax.experimental import pallas as pl
from jax.experimental.pallas import tpu as pltpu
from jax.sharding import PartitionSpec as P

BANDS = 432
LD = 32
SD = 16

MESH = pl.DeviceIdType.MESH
HIGH = lax.Precision.HIGHEST
LANES = 128


def blocks_of(bands):
    rows = [bands - start for start in range(0, bands, LANES)]
    offsets = [sum(rows[:i]) for i in range(len(rows))]
    return rows, offsets


alpha_lift = -1.586134342059924
beta_lift = -0.052980118572961
gamma_lift = 0.882911075530934
delta_lift = 0.443506852043971
scale_lift = 1.230174104914001
RIM = 4


def lift_list(values):
    evens, odds = values[0::2], values[1::2]
    odds = [o + alpha_lift * (e + f) for o, e, f in zip(odds[:-1], evens[:-1], evens[1:])]
    evens = [e + beta_lift * (o + q) for e, o, q in zip(evens[1:-1], odds[:-1], odds[1:])]
    odds = [o + gamma_lift * (e + f) for o, e, f in zip(odds[1:-1], evens[:-1], evens[1:])]
    evens = [e + delta_lift * (o + q) for e, o, q in zip(evens[1:-1], odds[:-1], odds[1:])]
    return [e * (1.0 / scale_lift) for e in evens], [o * scale_lift for o in odds[1:]]


def lift_lines(src, halo, dst, lines, width, ln):
    half = lines // 2
    for t in range(src.shape[0]):
        own = [src[t, i * width:(i + 1) * width] for i in range(lines)]
        got = [halo[t, i * width:(i + 1) * width] for i in range(RIM)]
        before = [jnp.where(ln == 0, own[RIM - i], got[i]) for i in range(RIM)]
        after = [jnp.where(ln == 0, got[i], own[lines - 2 - i]) for i in range(RIM)]
        low, high = lift_list(before + own + after)
        for i in range(half):
            dst[t, i * width:(i + 1) * width] = low[i]
            dst[t, (half + i) * width:(half + i + 1) * width] = high[i]


def rims(z, lines, width, left, right):
    for t in range(z.shape[0]):
        low = [z[t, pl.ds(s, lines, stride=width), :] for s in range(3)]
        top = [z[t, pl.ds(s, lines, stride=width), :] for s in range(width - 4, width)]
        left[t, :lines] = low[0]
        left[t, lines:] = low[0] + beta_lift * (low[1] + alpha_lift * (low[0] + low[2]))
        right[t, :lines] = top[3] + alpha_lift * top[2]
        right[t, lines:] = top[2] + beta_lift * (top[1] + alpha_lift * (top[0] + top[2]))


def lift_samples(z, from_left, from_right, lines, width, first, last, dests):
    half, n = lines // 2, width // 2
    for t in range(z.shape[0]):
        evens = [z[t, pl.ds(2 * i, lines, stride=width), :] for i in range(n)]
        odds = [z[t, pl.ds(2 * i + 1, lines, stride=width), :] for i in range(n)]
        beyond = jnp.where(last, evens[-1], from_right[t, :lines])
        odds1 = [o + alpha_lift * (e + f) for o, e, f in zip(odds, evens, evens[1:] + [beyond])]
        before = jnp.where(first, odds1[0], from_left[t, :lines] + alpha_lift * evens[0])
        evens1 = [e + beta_lift * (p + o) for e, p, o in zip(evens, [before] + odds1[:-1], odds1)]
        beyond = jnp.where(last, evens1[-1], from_right[t, lines:] + beta_lift * odds1[-1])
        odds2 = [o + gamma_lift * (e + f) for o, e, f in zip(odds1, evens1, evens1[1:] + [beyond])]
        outside = from_left[t, lines:] + beta_lift * before
        before = jnp.where(first, odds2[0], before + gamma_lift * (outside + evens1[0]))
        evens2 = [e + delta_lift * (p + o) for e, p, o in zip(evens1, [before] + odds2[:-1], odds2)]
        for i in range(n):
            low, high = evens2[i] * (1.0 / scale_lift), odds2[i] * scale_lift
            for (ref, base), value in zip(dests, (low[:half], low[half:], high[:half], high[half:])):
                ref[t, pl.ds(base + i, half, stride=n), :] = value


def split3(value):
    first = value.astype(jnp.bfloat16).astype(jnp.float32)
    rest = value - first
    second = rest.astype(jnp.bfloat16).astype(jnp.float32)
    return first, second, rest - second


def gram_kernel(samp, line, bands, lines, width, x_ref, o1_ref, o2_ref, o3_ref, o4_ref, t_ref, m, rest, corr, v1, v2, v3, z1, z2, z3, n1, n2, n3, el1, er1, el2, er2, el3, er3, fl1, fr1, fl2, fr2, fl3, fr3,
                l_send, l_recv, r_send, r_recv, xs, sums, sums_in, g, half_in,
                chunk_in, tot, s_send, s_recv, h_send, h_recv, c_send, c_recv, a_send, a_recv,
                b_send, b_recv):
    me, ln = lax.axis_index("samp"), lax.axis_index("line")
    devices = samp * line
    pixels = lines * width
    first, last = me == 0, me == samp - 1
    flat = me * line + ln
    packs = pixels // LANES
    padded = xs.shape[0]

    def peer(d):
        other = lax.rem(flat + d, devices)
        return {"samp": other // line, "line": lax.rem(other, line)}

    def line_copy(level, src, dst, tall, wide):
        rows = RIM * wide
        start = pl.multiple_of((1 - ln) * ((tall - RIM) * wide), 8)
        copy = pltpu.make_async_remote_copy(src.at[:, pl.ds(start, rows)], dst, l_send.at[level], l_recv.at[level],
                                            device_id={"line": 1 - ln}, device_id_type=MESH)
        copy.start()
        return copy

    def rim_copies(level, left, right, from_left, from_right):
        below = pltpu.make_async_remote_copy(left, from_right, r_send.at[level, 0], r_recv.at[level, 0],
                                             device_id={"samp": jnp.maximum(me - 1, 0)}, device_id_type=MESH)
        above = pltpu.make_async_remote_copy(right, from_left, r_send.at[level, 1], r_recv.at[level, 1],
                                             device_id={"samp": jnp.minimum(me + 1, samp - 1)}, device_id_type=MESH)

        @pl.when(me > 0)
        def _():
            below.start()

        @pl.when(me < samp - 1)
        def _():
            above.start()

        return below, above

    def rim_wait(pair):
        below, above = pair

        @pl.when(me > 0)
        def _():
            below.wait_send()
            above.wait_recv()

        @pl.when(me < samp - 1)
        def _():
            above.wait_send()
            below.wait_recv()

    for ref in (fl1, fr1, fl2, fr2, fl3, fr3):
        ref[...] = jnp.zeros_like(ref)
    barrier = pltpu.get_barrier_semaphore()
    for d in range(1, devices):
        pl.semaphore_signal(barrier, inc=1, device_id=peer(d), device_id_type=MESH)
    if padded > bands:
        xs[bands:, :] = jnp.zeros((padded - bands, pixels), jnp.float32)
    for q in range(packs):
        xs[0:bands, q * LANES:(q + 1) * LANES] = x_ref[pl.ds(q, bands, stride=packs), :]
    sums[...] = lax.dot_general(jnp.ones((8, pixels), jnp.float32), xs[...], (((1,), (1,)), ((), ())),
                                precision=HIGH, preferred_element_type=jnp.float32)[0:1]
    pl.semaphore_wait(barrier, devices - 1)
    copies = []
    for d in range(1, devices):
        copy = pltpu.make_async_remote_copy(sums, sums_in.at[d - 1], s_send.at[d - 1], s_recv.at[d - 1],
                                            device_id=peer(d), device_id_type=MESH)
        copy.start()
        copies.append(copy)
    sum_copies = copies
    local_mean = sums[...] / float(pixels)
    xs[...] = xs[...] - jnp.transpose(jnp.broadcast_to(local_mean, (8, padded)))[:, 0:1]
    rows, offsets = blocks_of(bands)
    for q, (count, offset) in enumerate(zip(rows, offsets)):
        g[offset:offset + count, :] = lax.dot_general(
            xs[q * LANES:q * LANES + count, :], xs[q * LANES:(q + 1) * LANES, :],
            (((1,), (1,)), ((), ())), precision=HIGH, preferred_element_type=jnp.float32)
    used = offsets[-1] + rows[-1]
    if g.shape[0] > used:
        g[used:, :] = jnp.zeros((g.shape[0] - used, LANES), jnp.float32)
    half = g.shape[0] // line
    chunk = half // samp
    copies = []
    for d in range(1, line):
        other = lax.rem(ln + d, line)
        copy = pltpu.make_async_remote_copy(
            g.at[pl.ds(pl.multiple_of(other * half, 8), half)], half_in.at[d - 1], h_send.at[d - 1],
            h_recv.at[d - 1], device_id={"line": other}, device_id_type=MESH)
        copy.start()
        copies.append(copy)
    for copy in copies:
        copy.wait()
    mine = pl.ds(pl.multiple_of(ln * half, 8), half)
    value = g[mine, :]
    for d in range(1, line):
        value = value + half_in[d - 1]
    g[mine, :] = value
    copies = []
    for d in range(1, samp):
        other = lax.rem(me + d, samp)
        copy = pltpu.make_async_remote_copy(
            g.at[pl.ds(pl.multiple_of(ln * half + other * chunk, 8), chunk)], chunk_in.at[d - 1],
            c_send.at[d - 1], c_recv.at[d - 1], device_id={"samp": other}, device_id_type=MESH)
        copy.start()
        copies.append(copy)
    for copy in sum_copies:
        copy.wait()
    total = sums[...]
    for d in range(1, devices):
        total = total + sums_in[d - 1]
    mean = total / float(pixels * devices)
    spread = jnp.concatenate([local_mean - mean] + [sums_in[d - 1] / float(pixels) - mean
                                                    for d in range(1, devices)], axis=0)
    shift = local_mean - mean
    for t in range(v1.shape[0]):
        v1[t] = jnp.transpose(xs[t * LANES:(t + 1) * LANES, :]) + shift[:, t * LANES:(t + 1) * LANES]
    lines1 = line_copy(0, v1, n1, lines, width)
    for q, (count, offset) in enumerate(zip(rows, offsets)):
        corr[offset:offset + count, :] = float(pixels) * lax.dot_general(
            spread, spread[:, q * LANES:(q + 1) * LANES], (((0,), (0,)), ((), ())), precision=HIGH,
            preferred_element_type=jnp.float32)[q * LANES:q * LANES + count]
    if g.shape[0] > used:
        corr[used:, :] = jnp.zeros((g.shape[0] - used, LANES), jnp.float32)
    lines1.wait()
    lift_lines(v1, n1, z1, lines, width, ln)
    rims(z1, lines, width, el1, er1)
    for copy in copies:
        copy.wait()
    own = pl.ds(pl.multiple_of(ln * half + me * chunk, 8), chunk)
    value = g[own, :] + corr[own, :]
    for d in range(1, samp):
        value = value + chunk_in[d - 1]
    tot[own, :] = value
    copies = []
    for d in range(1, samp):
        other = lax.rem(me + d, samp)
        copy = pltpu.make_async_remote_copy(tot.at[own], tot.at[own], a_send.at[d - 1], a_recv.at[d - 1],
                                            device_id={"samp": other}, device_id_type=MESH)
        copy.start()
        copies.append(copy)
    pair = rim_copies(0, el1, er1, fl1, fr1)
    for copy in copies:
        copy.wait()
    copies = []
    for d in range(1, line):
        other = lax.rem(ln + d, line)
        copy = pltpu.make_async_remote_copy(tot.at[mine], tot.at[mine], b_send.at[d - 1], b_recv.at[d - 1],
                                            device_id={"line": other}, device_id_type=MESH)
        copy.start()
        copies.append(copy)
    for copy in copies:
        copy.wait()
    wide = m.shape[1]
    rows, offsets = blocks_of(bands)
    diag = lax.broadcasted_iota(jnp.int32, (LANES, LANES), 0) == lax.broadcasted_iota(
        jnp.int32, (LANES, LANES), 1)
    scale = 1.0 / float(pixels * devices)
    trace = jnp.zeros((1, 1), jnp.float32)
    for q, offset in enumerate(offsets):
        size = min(LANES, rows[q])
        block = tot[offset:offset + size, :]
        kept = jnp.where(diag[:size], block, 0.0)
        trace = trace + jnp.sum(jnp.sum(kept, axis=0, keepdims=True), axis=1, keepdims=True)
    ridge = trace * scale * (0.01 / bands)
    for q, offset in enumerate(offsets):
        for b in range(q, len(rows)):
            size = min(LANES, rows[b])
            start = offset + (b - q) * LANES
            block = tot[start:start + size, :] * scale
            if b == q:
                low = jnp.where(diag[:size], block + ridge, block)
                m[q * LANES:q * LANES + size, q * LANES:(q + 1) * LANES] = low
            else:
                if size < LANES:
                    block = jnp.concatenate([block, jnp.zeros((LANES - size, LANES), jnp.float32)], axis=0)
                m[q * LANES:(q + 1) * LANES, b * LANES:(b + 1) * LANES] = jnp.transpose(block)
                m[b * LANES:b * LANES + size, q * LANES:(q + 1) * LANES] = block[:size]
    sub = lax.broadcasted_iota(jnp.int32, (8, LANES), 0)
    lane = lax.broadcasted_iota(jnp.int32, (8, LANES), 1)

    def eliminate(c):
        top = c * LANES
        span = bands - top

        def step(skip, j, carry):
            row = pl.multiple_of(top + 8 * j, 8)
            here = m[pl.ds(row, 8), top:top + LANES]
            small = pltpu.roll(here, lax.rem(LANES - 8 * j, LANES), 1)
            columns = [jnp.broadcast_to(small[:, b:b + 1], (8, LANES)) for b in range(8)]
            d = [[jnp.broadcast_to(columns[b][a:a + 1, :], (8, LANES)) if b <= a else None
                  for b in range(8)] for a in range(8)]
            low = [[None] * 8 for _ in range(8)]
            root = [None] * 8
            for b in range(8):
                root[b] = lax.rsqrt(d[b][b])
                for a in range(b + 1, 8):
                    low[a][b] = d[a][b] * root[b]
                for a in range(b + 1, 8):
                    for e in range(b + 1, a + 1):
                        d[a][e] = d[a][e] - low[a][b] * low[e][b]
            inv = [[None] * 8 for _ in range(8)]
            for b in range(8):
                inv[b][b] = root[b]
                for a in range(b + 1, 8):
                    acc = low[a][b] * inv[b][b]
                    for e in range(b + 1, a):
                        acc = acc + low[a][e] * inv[e][b]
                    inv[a][b] = -(acc * root[a])
            wcol = []
            for b in range(8):
                col = jnp.where(sub == b, inv[b][b], 0.0)
                for a in range(b + 1, 8):
                    col = jnp.where(sub == a, inv[a][b], col)
                wcol.append(col)
            tiles = []
            for t in range(wide // LANES):
                acc = None
                panel = m[pl.ds(row, 8), t * LANES:(t + 1) * LANES]
                for b in range(8):
                    term = wcol[b] * panel[b:b + 1, :]
                    acc = term if acc is None else acc + term
                if t == c:
                    for b in range(8):
                        acc = jnp.where(lane == 8 * j + b, wcol[b], acc)
                tiles.append(acc)
            r = jnp.concatenate(tiles, axis=1)
            m[pl.ds(row, 8), :] = r
            one, two, three = split3(r)
            right = jnp.concatenate([one, two, three, one, two, one], axis=0)
            cols = lax.broadcasted_iota(jnp.int32, (8, wide), 1)
            keep = (cols >= row + 8).astype(jnp.float32)
            l1, l2, l3 = one * keep, two * keep, three * keep
            left = jnp.concatenate([l1, l1, l1, l2, l2, l3], axis=0)[:, top:]
            update = lax.dot_general(
                left.astype(jnp.bfloat16), right.astype(jnp.bfloat16),
                (((0,), (0,)), ((), ())), preferred_element_type=jnp.float32)
            for t in range(wide // LANES):
                part = slice(t * LANES, (t + 1) * LANES)
                old = m[top + skip:bands, part]
                if t == c:
                    line_ids = lax.broadcasted_iota(jnp.int32, (span - skip, LANES), 0) + skip
                    lane_ids = lax.broadcasted_iota(jnp.int32, (span - skip, LANES), 1)
                    inside = (lane_ids >= 8 * j) & (lane_ids < 8 * j + 8) & (line_ids >= 8 * j + 8)
                    old = jnp.where(inside, 0.0, old)
                m[top + skip:bands, part] = old - update[skip:span, part]
            return carry

        steps = min(LANES, span) // 8
        middle = min(8, steps)
        lax.fori_loop(0, middle, functools.partial(step, 0), 0)
        if steps > middle:
            lax.fori_loop(middle, steps, functools.partial(step, 8 * middle), 0)
    eliminate(0)
    rim_wait(pair)
    h, w = lines // 2, width // 2
    one = h * w
    lift_samples(z1, fl1, fr1, lines, width, first, last, ((v2, 0), (t_ref, 0), (t_ref, one), (t_ref, 2 * one)))
    lines2 = line_copy(1, v2, n2, h, w)
    eliminate(1)
    lines2.wait()
    lift_lines(v2, n2, z2, h, w, ln)
    rims(z2, h, w, el2, er2)
    pair2 = rim_copies(1, el2, er2, fl2, fr2)
    eliminate(2)
    rim_wait(pair2)
    two, base2 = one // 4, 3 * one
    lift_samples(z2, fl2, fr2, h, w, first, last,
                 ((v3, 0), (t_ref, base2), (t_ref, base2 + two), (t_ref, base2 + 2 * two)))
    h, w = h // 2, w // 2
    lines3 = line_copy(2, v3, n3, h, w)
    lines3.wait()
    lift_lines(v3, n3, z3, h, w, ln)
    rims(z3, h, w, el3, er3)
    pair3 = rim_copies(2, el3, er3, fl3, fr3)
    for c in range(3, len(rows)):
        eliminate(c)
    rim_wait(pair3)
    three, base3 = two // 4, base2 + 3 * two
    lift_samples(z3, fl3, fr3, h, w, first, last,
                 ((t_ref, base3 + 3 * three), (t_ref, base3), (t_ref, base3 + three), (t_ref, base3 + 2 * three)))
    keep = lax.broadcasted_iota(jnp.int32, (bands, wide), 1) <= lax.broadcasted_iota(
        jnp.int32, (bands, wide), 0)
    m[...] = jnp.where(keep, m[...], 0.0)
    for q in range(t_ref.shape[1] // LANES):
        part = jnp.concatenate([t_ref[t, q * LANES:(q + 1) * LANES, :] for t in range(wide // LANES)], axis=1)
        out = lax.dot_general(m[...], part, (((1,), (1,)), ((), ())),
                              precision=HIGH, preferred_element_type=jnp.float32)
        if q < o1_ref.shape[0]:
            o1_ref[q] = out
        else:
            rest[...] = out


    def pack(dest, at, lane0, wide_out):
        group = LANES // wide_out
        count = bands // group
        pieces = [rest[pl.ds(b, count, stride=group), :][:, lane0:lane0 + wide_out] for b in range(group)]
        dest[at:at + count, :] = jnp.concatenate(pieces, axis=1)

    for i in range(3):
        pack(o2_ref, i * (o2_ref.shape[0] // 3), i * two, two)
        pack(o3_ref, i * (o3_ref.shape[0] // 3), 3 * two + i * three, three)
    pack(o4_ref, 0, 3 * two + 3 * three, three)


def gram_call(cube, bands, lines, width):
    pixels = lines * width
    samp, line = lax.axis_size("samp"), lax.axis_size("line")
    devices = samp * line
    rows, offsets = blocks_of(bands)
    used = offsets[-1] + rows[-1]
    unit = 8 * devices
    total = -(-used // unit) * unit
    padded = -(-bands // LANES) * LANES
    f32 = jnp.float32
    sem = pltpu.SemaphoreType.DMA
    return pl.pallas_call(
        functools.partial(gram_kernel, samp, line, bands, lines, width),
        out_shape=(jax.ShapeDtypeStruct((3, bands, LANES), f32),
                   jax.ShapeDtypeStruct((3 * bands * (pixels // 16) // LANES, LANES), f32),
                   jax.ShapeDtypeStruct((3 * bands * (pixels // 64) // LANES, LANES), f32),
                   jax.ShapeDtypeStruct((bands * (pixels // 64) // LANES, LANES), f32)),
        in_specs=[pl.BlockSpec(memory_space=pltpu.VMEM)],
        out_specs=(pl.BlockSpec(memory_space=pltpu.VMEM),) * 4,
        scratch_shapes=[
            pltpu.VMEM((padded // LANES, pixels, LANES), f32), pltpu.VMEM((bands, padded), f32),
            pltpu.VMEM((bands, LANES), f32), pltpu.VMEM((total, LANES), f32),
            *[pltpu.VMEM((padded // LANES, pixels // 4 ** i, LANES), f32) for i in (0, 1, 2)],
            *[pltpu.VMEM((padded // LANES, pixels // 4 ** i, LANES), f32) for i in (0, 1, 2)],
            *[pltpu.VMEM((padded // LANES, RIM * width // 2 ** i, LANES), f32) for i in (0, 1, 2)],
            *[pltpu.VMEM((padded // LANES, 2 * lines // 2 ** i, LANES), f32) for i in (0, 0, 1, 1, 2, 2)],
            *[pltpu.VMEM((padded // LANES, 2 * lines // 2 ** i, LANES), f32) for i in (0, 0, 1, 1, 2, 2)],
            sem((3,)), sem((3,)), sem((3, 2)), sem((3, 2)),
            pltpu.VMEM((padded, pixels), f32), pltpu.VMEM((1, padded), f32),
            pltpu.VMEM((devices - 1, 1, padded), f32), pltpu.VMEM((total, LANES), f32),
            pltpu.VMEM((line - 1, total // line, LANES), f32),
            pltpu.VMEM((samp - 1, total // devices, LANES), f32), pltpu.VMEM((total, LANES), f32),
            sem((devices - 1,)), sem((devices - 1,)), sem((line - 1,)), sem((line - 1,)),
            sem((samp - 1,)), sem((samp - 1,)), sem((samp - 1,)), sem((samp - 1,)),
            sem((line - 1,)), sem((line - 1,)),
        ],
        compiler_params=pltpu.CompilerParams(collective_id=0, has_side_effects=True),
    )(cube.reshape(-1, LANES))


def local(cube):
    return tuple(out.reshape(-1) for out in gram_call(cube, BANDS, LD, SD))


def solution(mesh):
    in_specs = (P(("groups", "samp", "line")),)
    out_specs = (
        P(("groups", "samp", "line")),
        P(("groups", "samp", "line")),
        P(("groups", "samp", "line")),
        P(("groups", "samp", "line")),
    )
    return jax.shard_map(local, mesh=mesh, in_specs=in_specs, out_specs=out_specs, check_vma=False)
```
